512 devices in a mesh: dp: 2 (over z_hi), ctx: 32 (over z_lo, y), tp: 8 (over x, core).
Axes of the slice: x: 4, y: 8, z: 8 (z_hi: 2, z_lo: 4; z = z_hi * 4 + z_lo), core: 2. Of those that a mesh axis runs over, the one named last changes fastest.
Arguments:
- left_stream: bfloat16 [2, 4096, 4096], P('dp', 'ctx', 'tp'), may hold values from -6 to 6
- outer_gate: bfloat16 [2, 4096, 4096], P('dp', 'ctx', 'tp'), may hold values from -6 to 6
- value_stream: bfloat16 [2, 4096, 4096], P('dp', 'ctx', 'tp'), may hold values from -6 to 6
- residual: bfloat16 [2, 4096, 4096], P('dp', 'ctx', 'tp'), may hold values from -36 to 36
- long_filter: float32 [256, 128], P('tp'), may hold values from -2 to 2
- skip_weight: float32 [4096], P('tp'), may hold values from -1 to 1
- norm_gain: float32 [4096], P('tp'), may hold values from 0.1 to 1.9
- normed_grad: bfloat16 [2, 4096, 4096], P('dp', 'ctx', 'tp'), may hold values from -6 to 6
- attn_queries: bfloat16 [2, 4096, 4096], P('dp', 'ctx', 'tp'), may hold values from -6 to 6
- attn_keys: bfloat16 [2, 4096, 4096], P('dp', 'ctx', 'tp'), may hold values from -6 to 6
- attn_values: bfloat16 [2, 4096, 4096], P('dp', 'ctx', 'tp'), may hold values from -6 to 6
- attended_grad: bfloat16 [2, 4096, 4096], P('dp', 'ctx', 'tp'), may hold values from -6 to 6
Outputs:
- normed: bfloat16 [2, 4096, 4096], P('dp', 'ctx', 'tp')
- grad_left: bfloat16 [2, 4096, 4096], P('dp', 'ctx', 'tp')
- grad_outer: bfloat16 [2, 4096, 4096], P('dp', 'ctx', 'tp')
- grad_value: bfloat16 [2, 4096, 4096], P('dp', 'ctx', 'tp')
- grad_residual: bfloat16 [2, 4096, 4096], P('dp', 'ctx', 'tp')
- grad_filter: float32 [256, 128], P('tp')
- grad_skip: float32 [4096], P('tp')
- grad_gain: float32 [4096], P('tp')
- attended: bfloat16 [2, 4096, 4096], P('dp', 'ctx', 'tp')
- grad_queries: bfloat16 [2, 4096, 4096], P('dp', 'ctx', 'tp')
- grad_keys: bfloat16 [2, 4096, 4096], P('dp', 'ctx', 'tp')
- grad_values: bfloat16 [2, 4096, 4096], P('dp', 'ctx', 'tp')
The draws below stay inside these ranges and needn't reach their ends.
All inputs are finite; a program needn't handle non-finite values.
Results may differ from the reference program's by a relative error of at most 0.024.
Values may be sent and summed in bfloat16 or wider, within the bound.
A program may use at most 128 MiB of HBM per device.

```python
import math
import jax
import jax.numpy as jnp
from jax import lax

TAPS = 128
GROUP = 16
CH = 4096
HEADS = 32
HEAD_DIM = 128
SEQ_LEN = 4096
SEQS = 2
FILTERS = 256


def draw_residual(key, part):
    base_key = jax.random.fold_in(key, 0)
    base = jax.random.truncated_normal(base_key, -4.0, 4.0, (SEQS, SEQ_LEN, CH), jnp.float32)
    column = 1.0 + 2.0 * jnp.arange(CH, dtype=jnp.float32) / CH
    return (base * column).astype(jnp.bfloat16)


def draw_long_filter(key, part):
    base_key, rate_key = jax.random.split(key)
    base = jax.random.truncated_normal(base_key, -4.0, 4.0, (FILTERS, TAPS), jnp.float32)
    lowest = 0.2
    highest = 5.0
    rate = jnp.exp(jax.random.uniform(rate_key, (FILTERS, 1), jnp.float32, math.log(lowest), math.log(highest))) / TAPS
    position = jnp.arange(TAPS, dtype=jnp.float32)
    return base * jnp.exp(-position[None, :] * rate) * (1.5 / math.sqrt(TAPS))


def attention_pair(key):
    base = jax.random.fold_in(key, 11)
    query_key, key_key = jax.random.split(base, 2)
    shape = (SEQS, SEQ_LEN, HEADS * HEAD_DIM)
    queries = jax.random.truncated_normal(query_key, -6.0, 6.0, shape, jnp.float32)
    keys_out = jax.random.truncated_normal(key_key, -6.0, 6.0, shape, jnp.float32)
    return (queries, keys_out)


def draw_attn_queries(key, part):
    return attention_pair(key)[0].astype(jnp.bfloat16)


def draw_attn_keys(key, part):
    return attention_pair(key)[1].astype(jnp.bfloat16)


def steps_of(stream_key, extent, shards, low, high):
    def one(dim, parts):
        steps = jax.random.uniform(jax.random.fold_in(jax.random.fold_in(stream_key, 6), dim), (parts,), jnp.float32, low / len(shards), high / len(shards))
        return jnp.repeat(jnp.exp(steps), extent[dim] // parts).reshape((-1,) + (1,) * (len(extent) - dim - 1))

    gain = one(*shards[0])
    for cut in shards[1:]:
        gain = gain * one(*cut)
    return gain


def normal_values(key, shape, scale, most, cuts=(), kind=jnp.bfloat16):
    loudness = steps_of(key, shape, cuts, -0.22, 0.18) if cuts else 1.0
    values = jax.random.normal(key, shape, jnp.float32) * scale * loudness
    return jnp.minimum(jnp.maximum(values, -most), most).astype(kind)


def setup_inputs(seed: int = 0) -> dict:
    seeds = jax.random.split(jax.random.key(seed), 13)
    return {
        "left_stream": normal_values(seeds[0], (SEQS, SEQ_LEN, CH), 1.0, 6.0, ((0, 2), (1, 32), (2, 8))),
        "outer_gate": normal_values(seeds[1], (SEQS, SEQ_LEN, CH), 1.0, 6.0, ((0, 2), (1, 32), (2, 8))),
        "value_stream": normal_values(seeds[2], (SEQS, SEQ_LEN, CH), 1.0, 6.0, ((0, 2), (1, 32), (2, 8))),
        "residual": draw_residual(jax.random.fold_in(seeds[12], 71), 0),
        "long_filter": draw_long_filter(jax.random.fold_in(seeds[12], 71), 0),
        "skip_weight": jnp.clip(jax.random.uniform(seeds[5], (CH,), jnp.float32, -1.0, 1.0) * steps_of(seeds[5], (CH,), ((0, 8),), -0.4, 0.0), -1.0, 1.0),
        "norm_gain": jnp.clip(1.0 + 0.18 * jax.random.normal(seeds[6], (CH,), jnp.float32), 0.1, 1.9),
        "normed_grad": normal_values(seeds[7], (SEQS, SEQ_LEN, CH), 1.0, 6.0, ((0, 2), (1, 32), (2, 8))),
        "attn_queries": draw_attn_queries(jax.random.fold_in(seeds[12], 71), 0),
        "attn_keys": draw_attn_keys(jax.random.fold_in(seeds[12], 71), 0),
        "attn_values": normal_values(seeds[10], (SEQS, SEQ_LEN, HEADS * HEAD_DIM), 1.0, 6.0, ((0, 2), (1, 32), (2, 8))),
        "attended_grad": normal_values(seeds[11], (SEQS, SEQ_LEN, HEADS * HEAD_DIM), 1.0, 6.0, ((0, 2), (1, 32), (2, 8))),
    }


def forward_filter(signal, per_channel):
    length = signal.shape[1]
    padded = jnp.pad(signal, ((0, 0), (TAPS - 1, 0), (0, 0)))

    def add_tap(number, total):
        window = lax.dynamic_slice_in_dim(padded, TAPS - 1 - number, length, 1)
        column = lax.dynamic_index_in_dim(per_channel, number, 1, keepdims=False)
        return total + column[None, None, :] * window
    return lax.fori_loop(0, TAPS, add_tap, jnp.zeros_like(signal))

def backward_filter(signal, per_channel):
    length = signal.shape[1]
    padded = jnp.pad(signal, ((0, 0), (0, TAPS - 1), (0, 0)))

    def add_tap(number, total):
        window = lax.dynamic_slice_in_dim(padded, number, length, 1)
        column = lax.dynamic_index_in_dim(per_channel, number, 1, keepdims=False)
        return total + column[None, None, :] * window
    return lax.fori_loop(0, TAPS, add_tap, jnp.zeros_like(signal))

def head_pass(inputs):
    queries, keys_in, values_in, grad_out = inputs
    length = queries.shape[0]
    scale = HEAD_DIM ** (-0.5)
    scores = jnp.dot(queries, keys_in.T, preferred_element_type=jnp.float32) * scale
    position = jnp.arange(length, dtype=jnp.int32)
    allowed = position[None, :] <= position[:, None]
    scores = jnp.where(allowed, scores, -jnp.inf)
    highest = lax.optimization_barrier(jnp.max(scores, axis=1, keepdims=True))
    log_norm = highest + jnp.log(lax.optimization_barrier(jnp.sum(jnp.exp(scores - highest), axis=1, keepdims=True)))
    weights = jnp.exp(scores - log_norm).astype(jnp.bfloat16)
    attended = jnp.dot(weights, values_in, preferred_element_type=jnp.float32).astype(jnp.bfloat16)
    delta = lax.optimization_barrier(jnp.sum(grad_out.astype(jnp.float32) * attended.astype(jnp.float32), axis=1, keepdims=True))
    value_dots = jnp.dot(grad_out, values_in.T, preferred_element_type=jnp.float32)
    score_grad = (weights.astype(jnp.float32) * (value_dots - delta)).astype(jnp.bfloat16)
    query_grad = (jnp.dot(score_grad, keys_in, preferred_element_type=jnp.float32) * scale).astype(jnp.bfloat16)
    key_grad = (jnp.dot(score_grad.T, queries, preferred_element_type=jnp.float32) * scale).astype(jnp.bfloat16)
    value_grad = jnp.dot(weights.T, grad_out, preferred_element_type=jnp.float32).astype(jnp.bfloat16)
    return (attended, query_grad, key_grad, value_grad)

def split_heads(array):
    return array.reshape(SEQS, SEQ_LEN, HEADS, HEAD_DIM).transpose(0, 2, 1, 3).reshape(SEQS * HEADS, SEQ_LEN, HEAD_DIM)

def join_heads(array):
    return array.reshape(SEQS, HEADS, SEQ_LEN, HEAD_DIM).transpose(0, 2, 1, 3).reshape(SEQS, SEQ_LEN, HEADS * HEAD_DIM)

def reference(left_stream, outer_gate, value_stream, residual, long_filter, skip_weight, norm_gain, normed_grad, attn_queries, attn_keys, attn_values, attended_grad):
    left_values = left_stream.astype(jnp.float32)
    value_values = value_stream.astype(jnp.float32)
    gate_values = outer_gate.astype(jnp.float32)
    product = (left_values * value_values).astype(jnp.bfloat16)
    product_wide = product.astype(jnp.float32)
    per_channel = jnp.repeat(long_filter, GROUP, axis=0)
    mixed = forward_filter(product_wide, per_channel) + skip_weight * product_wide
    stream = residual.astype(jnp.float32) + gate_values * mixed
    inv_rms = lax.rsqrt(lax.optimization_barrier(jnp.mean(stream * stream, axis=2, keepdims=True)) + 1e-06)
    scaled = stream * inv_rms
    normed = (scaled * norm_gain).astype(jnp.bfloat16)
    upstream = normed_grad.astype(jnp.float32)
    gain_grad = upstream * norm_gain
    norm_dot = lax.optimization_barrier(jnp.sum(gain_grad * scaled, axis=2, keepdims=True))
    stream_grad = inv_rms * (gain_grad - scaled * norm_dot / CH)
    grad_residual = stream_grad.astype(jnp.bfloat16)
    grad_outer = (stream_grad * mixed).astype(jnp.bfloat16)
    gated = (stream_grad * gate_values).astype(jnp.bfloat16)
    gated_wide = gated.astype(jnp.float32)
    product_grad = backward_filter(gated_wide, per_channel) + skip_weight * gated_wide
    grad_left = (product_grad * value_values).astype(jnp.bfloat16)
    grad_value = (product_grad * left_values).astype(jnp.bfloat16)
    leading = jnp.pad(product_wide, ((0, 0), (TAPS - 1, 0), (0, 0)))

    def tap_grad(number):
        window = lax.dynamic_slice_in_dim(leading, TAPS - 1 - number, SEQ_LEN, 1)
        return lax.optimization_barrier(jnp.sum(gated_wide * window, axis=(0, 1)))
    per_tap = lax.map(tap_grad, jnp.arange(TAPS, dtype=jnp.int32))
    grad_filter = lax.optimization_barrier(jnp.sum(per_tap.T.reshape(FILTERS, GROUP, TAPS), axis=1))
    grad_skip = lax.optimization_barrier(jnp.sum(gated_wide * product_wide, axis=(0, 1)))
    grad_gain = lax.optimization_barrier(jnp.sum(upstream * scaled, axis=(0, 1)))
    stacked = (split_heads(attn_queries), split_heads(attn_keys), split_heads(attn_values), split_heads(attended_grad))
    attended, grad_queries, grad_keys, grad_values = lax.map(head_pass, stacked)
    return (normed, grad_left, grad_outer, grad_value, grad_residual, grad_filter, grad_skip, grad_gain, join_heads(attended), join_heads(grad_queries), join_heads(grad_keys), join_heads(grad_values))
```

```python
import math

import jax
import jax.numpy as jnp
from jax import lax
from jax.experimental import pallas as pl
from jax.experimental.pallas import tpu as pltpu
from jax.sharding import PartitionSpec as P

HEAD_DIM = 128
LANES = 128
LOG2E = math.log2(math.e)
F32 = jnp.float32
BF16 = jnp.bfloat16
VMEM = pltpu.VMEM


def passed_along(value, axis, steps):
    count = lax.axis_size(axis)
    initial, last = (max(0, -steps), min(count, count - steps))
    return lax.ppermute(value, axis, [(source, source + steps) for source in range(initial, last)])


def dot_nt(a, b):
    return lax.dot_general(a, b, (((1,), (1,)), ((), ())), preferred_element_type=F32)


def dot_nn(a, b):
    return lax.dot_general(a, b, (((1,), (0,)), ((), ())), preferred_element_type=F32)


def whole(count):
    return [pl.BlockSpec(memory_space=VMEM) for _ in range(count)]


def row_of(column):
    return jnp.transpose(jnp.broadcast_to(column, (column.shape[0], LANES)))[0:1]


def query_kernel(place_ref, own_ref, kv_ref, att_ref, dq_ref, stat_ref, s_ref, p_ref):
    place = place_ref[0]
    ring, strips, _, rows, depth = kv_ref.shape
    span = ring * rows
    factor = HEAD_DIM ** (-0.5) * LOG2E
    line = lax.broadcasted_iota(jnp.int32, (rows, span), 0) + place * rows
    allowed = lax.broadcasted_iota(jnp.int32, (rows, span), 1) <= line
    tops = [None] * strips
    for zk in range(strips):
        key = kv_ref[:, zk, 0].reshape(span, depth)
        query = own_ref[zk:, 0].reshape((strips - zk) * rows, depth)
        scores = dot_nt(query, key) * factor
        for zq in range(zk, strips):
            part = scores[(zq - zk) * rows : (zq - zk + 1) * rows]
            if zq == zk:
                part = jnp.where(allowed, part, -1e30)
            s_ref[zq * rows : (zq + 1) * rows, zk * span : (zk + 1) * span] = part
            top = jnp.max(part, axis=1, keepdims=True)
            tops[zq] = top if zk == 0 else jnp.maximum(tops[zq], top)
    totals = [jnp.zeros((rows, 1), F32) for _ in range(strips)]
    outs = [jnp.zeros((rows, depth), F32) for _ in range(strips)]
    for zk in range(strips):
        columns = slice(zk * span, (zk + 1) * span)
        for zq in range(zk, strips):
            lines = slice(zq * rows, (zq + 1) * rows)
            power = jnp.exp2(s_ref[lines, columns] - tops[zq])
            totals[zq] = totals[zq] + jnp.sum(power, axis=1, keepdims=True)
            p_ref[lines, columns] = power.astype(BF16)
        value = kv_ref[:, zk, 1].reshape(span, depth)
        added = dot_nn(p_ref[zk * rows :, columns], value)
        for zq in range(zk, strips):
            outs[zq] = outs[zq] + added[(zq - zk) * rows : (zq - zk + 1) * rows]
    inverses, deltas = ([], [])
    for zq in range(strips):
        inverse = 1.0 / totals[zq]
        attended = (outs[zq] * inverse).astype(BF16)
        att_ref[zq] = attended
        delta = jnp.sum(
            own_ref[zq, 1].astype(F32) * attended.astype(F32), axis=1, keepdims=True
        )
        stat_ref[zq, 0:1] = row_of(tops[zq] + jnp.log(totals[zq]) * LOG2E)
        stat_ref[zq, 1:2] = row_of(delta)
        inverses.append(inverse)
        deltas.append(delta)
    grads = [jnp.zeros((rows, depth), F32) for _ in range(strips)]
    for zk in range(strips):
        columns = slice(zk * span, (zk + 1) * span)
        key = kv_ref[:, zk, 0].reshape(span, depth)
        value = kv_ref[:, zk, 1].reshape(span, depth)
        out_grad = own_ref[zk:, 1].reshape((strips - zk) * rows, depth)
        dots = dot_nt(out_grad, value)
        parts = []
        for zq in range(zk, strips):
            lines = slice(zq * rows, (zq + 1) * rows)
            here = dots[(zq - zk) * rows : (zq - zk + 1) * rows]
            parts.append((p_ref[lines, columns].astype(F32) * (here - deltas[zq])).astype(BF16))
        added = dot_nn(jnp.concatenate(parts, axis=0), key)
        for zq in range(zk, strips):
            grads[zq] = grads[zq] + added[(zq - zk) * rows : (zq - zk + 1) * rows]
    for zq in range(strips):
        dq_ref[zq] = (grads[zq] * (inverses[zq] * HEAD_DIM ** (-0.5))).astype(BF16)


def key_kernel(place_ref, own_ref, qd_ref, stat_ref, dk_ref, dv_ref):
    place = place_ref[0]
    ring, strips, _, rows, depth = qd_ref.shape
    span = ring * rows
    factor = HEAD_DIM ** (-0.5) * LOG2E
    line = lax.broadcasted_iota(jnp.int32, (rows, span), 0) + place * rows
    allowed = lax.broadcasted_iota(jnp.int32, (rows, span), 1) >= line
    key_sums = [jnp.zeros((rows, depth), F32) for _ in range(strips)]
    value_sums = [jnp.zeros((rows, depth), F32) for _ in range(strips)]
    for zq in range(strips):
        count = zq + 1
        query = qd_ref[:, zq, 0].reshape(span, depth)
        out_grad = qd_ref[:, zq, 1].reshape(span, depth)
        norm = jnp.concatenate([stat_ref[r, zq, 0:1] for r in range(ring)], axis=1)
        delta = jnp.concatenate([stat_ref[r, zq, 1:2] for r in range(ring)], axis=1)
        key = own_ref[:count, 0].reshape(count * rows, depth)
        value = own_ref[:count, 1].reshape(count * rows, depth)
        scores = dot_nt(key, query) * factor - norm
        last = jnp.where(allowed, scores[zq * rows :], -1e30)
        if zq:
            scores = jnp.concatenate([scores[: zq * rows], last], axis=0)
        else:
            scores = last
        weights = jnp.exp2(scores).astype(BF16)
        dots = dot_nt(value, out_grad)
        score_grad = (weights.astype(F32) * (dots - delta)).astype(BF16)
        value_added = dot_nn(weights, out_grad)
        key_added = dot_nn(score_grad, query)
        for zk in range(count):
            lines = slice(zk * rows, (zk + 1) * rows)
            value_sums[zk] = value_sums[zk] + value_added[lines]
            key_sums[zk] = key_sums[zk] + key_added[lines]
    for zk in range(strips):
        dk_ref[zk] = (key_sums[zk] * HEAD_DIM ** (-0.5)).astype(BF16)
        dv_ref[zk] = value_sums[zk].astype(BF16)


def fill_phases(first, second, ext_ref, phase_ref):
    rows = first.shape[0]
    ext_ref[:rows] = first
    ext_ref[rows:] = second
    for r in range(8):
        phase_ref[r] = ext_ref[r : r + 2 * rows - 8]


def mix_kernel(
    left_ref, value_ref, before_ref, gate_ref, residual_ref, upstream_ref, taps_ref, skip_ref,
    gain_ref, mixed_ref, stream_ref, sums_ref, ext_ref, phase_ref,
):
    rows = left_ref.shape[0]
    taps = taps_ref.shape[0]
    product = (left_ref[...].astype(F32) * value_ref[...].astype(F32)).astype(BF16).astype(F32)
    fill_phases(before_ref[...].astype(F32), product, ext_ref, phase_ref)
    mixed = (taps_ref[0:1] + skip_ref[...]) * product
    for tap in range(1, taps):
        a, r = divmod(rows - tap, 8)
        mixed = mixed + taps_ref[tap : tap + 1] * phase_ref[r, 8 * a : 8 * a + rows]
    stream = residual_ref[...].astype(F32) + gate_ref[...].astype(F32) * mixed
    mixed_ref[...] = mixed
    stream_ref[...] = stream
    upstream = upstream_ref[...].astype(F32) * gain_ref[...]

    @pl.when(pl.program_id(0) == 0)
    def _():
        sums_ref[...] = jnp.zeros_like(sums_ref)

    sums_ref[0] += stream * stream
    sums_ref[1] += upstream * stream


def norm_kernel(
    upstream_ref, gate_ref, mixed_ref, stream_ref, gain_ref, totals_ref,
    normed_ref, residual_grad_ref, outer_grad_ref, gated_ref, gain_grad_ref, *, width,
):
    inv_rms = lax.rsqrt(totals_ref[:, 0:1] * (1.0 / width) + 1e-06)
    norm_dot = totals_ref[:, 1:2] * inv_rms * (1.0 / width)
    gain = gain_ref[...]
    upstream = upstream_ref[...].astype(F32)
    scaled = stream_ref[...] * inv_rms
    normed_ref[...] = (scaled * gain).astype(BF16)
    gain_grad_ref[...] = jnp.sum(upstream * scaled, axis=0, keepdims=True)
    stream_grad = inv_rms * (upstream * gain - scaled * norm_dot)
    residual_grad_ref[...] = stream_grad.astype(BF16)
    outer_grad_ref[...] = (stream_grad * mixed_ref[...]).astype(BF16)
    gated_ref[...] = (stream_grad * gate_ref[...].astype(F32)).astype(BF16)


def back_kernel(
    left_ref, value_ref, before_ref, gated_ref, after_ref, taps_ref, skip_ref,
    left_grad_ref, value_grad_ref, filter_ref, skip_grad_ref, ext_ref, phase_ref,
):
    rows = left_ref.shape[0]
    taps = taps_ref.shape[0]
    left = left_ref[...].astype(F32)
    value = value_ref[...].astype(F32)
    product = (left * value).astype(BF16).astype(F32)
    gated = gated_ref[...].astype(F32)
    fill_phases(gated, after_ref[...].astype(F32), ext_ref, phase_ref)
    grad = (skip_ref[...] + taps_ref[0:1]) * gated
    for tap in range(1, taps):
        a, r = divmod(tap, 8)
        grad = grad + taps_ref[tap : tap + 1] * phase_ref[r, 8 * a : 8 * a + rows]
    left_grad_ref[...] = (grad * value).astype(BF16)
    value_grad_ref[...] = (grad * left).astype(BF16)
    fill_phases(before_ref[...].astype(F32), product, ext_ref, phase_ref)
    direct = jnp.sum(gated * product, axis=0, keepdims=True)
    skip_grad_ref[...] = direct
    filter_ref[0:1] = direct
    for tap in range(1, taps):
        a, r = divmod(rows - tap, 8)
        filter_ref[tap : tap + 1] = jnp.sum(
            gated * phase_ref[r, 8 * a : 8 * a + rows], axis=0, keepdims=True
        )


def shape_of(shape, dtype):
    return jax.ShapeDtypeStruct(shape, dtype)


def shards(
    left_stream,
    outer_gate,
    value_stream,
    residual,
    long_filter,
    skip_weight,
    norm_gain,
    normed_grad,
    attn_queries,
    attn_keys,
    attn_values,
    attended_grad,
):
    rows = left_stream.shape[1]
    channels = left_stream.shape[2]
    groups, taps = long_filter.shape
    per_group = channels // groups
    width = channels * lax.axis_size("tp")
    heads = attn_queries.shape[2] // HEAD_DIM
    devices = lax.axis_size("ctx")
    ring = devices // heads
    index = lax.axis_index("ctx")
    place = (index % ring).astype(jnp.int32).reshape(1)
    across = [[strip * ring + spot for strip in range(heads)] for spot in range(ring)]
    along = [[strip * ring + spot for spot in range(ring)] for strip in range(heads)]

    stacked = jnp.stack([attn_keys[0], attn_values[0], attn_queries[0], attended_grad[0]])
    stacked = stacked.reshape(4, rows, heads, HEAD_DIM).transpose(2, 0, 1, 3)
    own = lax.all_to_all(stacked, "ctx", 0, 0, axis_index_groups=across, tiled=True)
    own_kv, own_qd = (own[:, :2], own[:, 2:])
    all_kv = lax.all_gather(own_kv, "ctx", axis=0, axis_index_groups=along, tiled=False)
    all_qd = lax.all_gather(own_qd, "ctx", axis=0, axis_index_groups=along, tiled=False)

    left, value, gate = (left_stream[0], value_stream[0], outer_gate[0])
    upstream = normed_grad[0]
    product = (left.astype(F32) * value.astype(F32)).astype(BF16)
    before = passed_along(product, "ctx", 1)
    taps_rows = jnp.repeat(long_filter.T, per_group, axis=1)
    skip, gain = (skip_weight[None, :], norm_gain[None, :])
    grid = (channels // LANES,)
    block = pl.BlockSpec((rows, LANES), lambda j: (0, j))
    tap_block = pl.BlockSpec((taps, LANES), lambda j: (0, j))
    line = pl.BlockSpec((1, LANES), lambda j: (0, j))
    phases = [VMEM((2 * rows, LANES), F32), VMEM((8, 2 * rows - 8, LANES), F32)]
    size = rows * channels
    mixed, stream, sums = pl.pallas_call(
        mix_kernel,
        grid=grid,
        in_specs=[block] * 6 + [tap_block, line, line],
        out_specs=[block, block, pl.BlockSpec((2, rows, LANES), lambda j: (0, 0, 0))],
        out_shape=[
            shape_of((rows, channels), F32),
            shape_of((rows, channels), F32),
            shape_of((2, rows, LANES), F32),
        ],
        scratch_shapes=phases,
        cost_estimate=pl.CostEstimate(
            flops=2 * taps * size, bytes_accessed=20 * size, transcendentals=0
        ),
        name="mix",
    )(left, value, before, gate, residual[0], upstream, taps_rows, skip, gain)
    totals = lax.psum(jnp.sum(sums, axis=2), "tp").T
    normed, grad_residual, grad_outer, gated, gain_part = pl.pallas_call(
        lambda *refs: norm_kernel(*refs, width=width),
        in_specs=whole(6),
        out_specs=whole(5),
        out_shape=[shape_of((rows, channels), BF16)] * 4 + [shape_of((1, channels), F32)],
        cost_estimate=pl.CostEstimate(
            flops=20 * size, bytes_accessed=20 * size, transcendentals=0
        ),
        name="norm",
    )(upstream, gate, mixed, stream, gain, totals)
    after = passed_along(gated, "ctx", -1)
    grad_left, grad_value, filter_rows, skip_part = pl.pallas_call(
        back_kernel,
        grid=grid,
        in_specs=[block] * 5 + [tap_block, line],
        out_specs=[block, block, tap_block, line],
        out_shape=[
            shape_of((rows, channels), BF16),
            shape_of((rows, channels), BF16),
            shape_of((taps, channels), F32),
            shape_of((1, channels), F32),
        ],
        scratch_shapes=phases,
        cost_estimate=pl.CostEstimate(
            flops=4 * taps * size, bytes_accessed=20 * size, transcendentals=0
        ),
        name="back",
    )(left, value, before, gated, after, taps_rows, skip)
    member = (
        jnp.arange(channels, dtype=jnp.int32)[None, :] // per_group
        == jnp.arange(groups, dtype=jnp.int32)[:, None]
    ).astype(F32)
    filter_part = lax.dot_general(
        member, filter_rows, (((1,), (1,)), ((), ())), precision=lax.Precision.HIGHEST
    )
    small = jnp.concatenate(
        [filter_part.reshape(-1), skip_part.reshape(-1), gain_part.reshape(-1)]
    )
    small = lax.psum(small, ("dp", "ctx"))
    cut = groups * taps
    filter_sum = small[:cut].reshape(groups, taps)
    skip_sum, gain_sum = (small[cut : cut + channels], small[cut + channels :])

    smem = pl.BlockSpec(memory_space=pltpu.SMEM)
    blocks = (heads, rows, HEAD_DIM)
    pairs = heads * (heads + 1) // 2 * rows * ring * rows
    attended, grad_queries, stats = pl.pallas_call(
        query_kernel,
        in_specs=[smem] + whole(2),
        out_specs=whole(3),
        out_shape=[shape_of(blocks, BF16), shape_of(blocks, BF16), shape_of((heads, 2, rows), F32)],
        scratch_shapes=[
            VMEM((heads * rows, devices * rows), F32),
            VMEM((heads * rows, devices * rows), BF16),
        ],
        cost_estimate=pl.CostEstimate(
            flops=8 * HEAD_DIM * pairs, bytes_accessed=3 << 20, transcendentals=pairs
        ),
        name="query",
    )(place, own_qd, all_kv)
    all_stats = lax.all_gather(stats, "ctx", axis=0, axis_index_groups=along, tiled=False)
    grad_keys, grad_values = pl.pallas_call(
        key_kernel,
        in_specs=[smem] + whole(3),
        out_specs=whole(2),
        out_shape=[shape_of(blocks, BF16)] * 2,
        cost_estimate=pl.CostEstimate(
            flops=8 * HEAD_DIM * pairs, bytes_accessed=3 << 20, transcendentals=pairs
        ),
        name="key",
    )(place, own_kv, all_qd, all_stats)
    back = jnp.stack([attended, grad_queries, grad_keys, grad_values], axis=1)
    back = lax.all_to_all(back, "ctx", 0, 0, axis_index_groups=across, tiled=True)
    back = back.transpose(1, 2, 0, 3).reshape(4, rows, heads * HEAD_DIM)
    return (
        normed[None],
        grad_left[None],
        grad_outer[None],
        grad_value[None],
        grad_residual[None],
        filter_sum,
        skip_sum,
        gain_sum,
        back[0:1],
        back[1:2],
        back[2:3],
        back[3:4],
    )


def solution(mesh):
    in_specs = (
        P("dp", "ctx", "tp"),
        P("dp", "ctx", "tp"),
        P("dp", "ctx", "tp"),
        P("dp", "ctx", "tp"),
        P("tp", None),
        P("tp"),
        P("tp"),
        P("dp", "ctx", "tp"),
        P("dp", "ctx", "tp"),
        P("dp", "ctx", "tp"),
        P("dp", "ctx", "tp"),
        P("dp", "ctx", "tp"),
    )
    out_specs = (
        P("dp", "ctx", "tp"),
        P("dp", "ctx", "tp"),
        P("dp", "ctx", "tp"),
        P("dp", "ctx", "tp"),
        P("dp", "ctx", "tp"),
        P("tp", None),
        P("tp"),
        P("tp"),
        P("dp", "ctx", "tp"),
        P("dp", "ctx", "tp"),
        P("dp", "ctx", "tp"),
        P("dp", "ctx", "tp"),
    )
    return jax.shard_map(shards, mesh=mesh, in_specs=in_specs, out_specs=out_specs, check_vma=False)
```

```python
import math

import jax
import jax.numpy as jnp
from jax import lax
from jax.experimental import pallas as pl
from jax.experimental.pallas import tpu as pltpu
from jax.sharding import PartitionSpec as P

HEAD_DIM = 128
LANES = 128
LOG2E = math.log2(math.e)
F32 = jnp.float32
BF16 = jnp.bfloat16
VMEM = pltpu.VMEM


def passed_along(value, axis, steps):
    count = lax.axis_size(axis)
    initial, last = (max(0, -steps), min(count, count - steps))
    return lax.ppermute(value, axis, [(source, source + steps) for source in range(initial, last)])


def dot_nt(a, b):
    return lax.dot_general(a, b, (((1,), (1,)), ((), ())), preferred_element_type=F32)


def dot_nn(a, b):
    return lax.dot_general(a, b, (((1,), (0,)), ((), ())), preferred_element_type=F32)


def whole(count):
    return [pl.BlockSpec(memory_space=VMEM) for _ in range(count)]


def row_of(column):
    return jnp.transpose(jnp.broadcast_to(column, (column.shape[0], LANES)))[0:1]


def query_kernel(place_ref, own_ref, kv_ref, att_ref, dq_ref, stat_ref, s_ref, p_ref):
    place = place_ref[0]
    ring, strips, _, rows, depth = kv_ref.shape
    span = ring * rows
    factor = HEAD_DIM ** (-0.5) * LOG2E
    line = lax.broadcasted_iota(jnp.int32, (rows, span), 0) + place * rows
    allowed = lax.broadcasted_iota(jnp.int32, (rows, span), 1) <= line
    tops = [None] * strips
    for zk in range(strips):
        key = kv_ref[:, zk, 0].reshape(span, depth)
        query = own_ref[zk:, 0].reshape((strips - zk) * rows, depth)
        scores = dot_nt(query, key) * factor
        for zq in range(zk, strips):
            part = scores[(zq - zk) * rows : (zq - zk + 1) * rows]
            if zq == zk:
                part = jnp.where(allowed, part, -1e30)
            s_ref[zq * rows : (zq + 1) * rows, zk * span : (zk + 1) * span] = part
            top = jnp.max(part, axis=1, keepdims=True)
            tops[zq] = top if zk == 0 else jnp.maximum(tops[zq], top)
    totals = [jnp.zeros((rows, 1), F32) for _ in range(strips)]
    outs = [jnp.zeros((rows, depth), F32) for _ in range(strips)]
    for zk in range(strips):
        columns = slice(zk * span, (zk + 1) * span)
        for zq in range(zk, strips):
            lines = slice(zq * rows, (zq + 1) * rows)
            power = jnp.exp2(s_ref[lines, columns] - tops[zq])
            totals[zq] = totals[zq] + jnp.sum(power, axis=1, keepdims=True)
            p_ref[lines, columns] = power.astype(BF16)
        value = kv_ref[:, zk, 1].reshape(span, depth)
        added = dot_nn(p_ref[zk * rows :, columns], value)
        for zq in range(zk, strips):
            outs[zq] = outs[zq] + added[(zq - zk) * rows : (zq - zk + 1) * rows]
    inverses, deltas = ([], [])
    for zq in range(strips):
        inverse = 1.0 / totals[zq]
        attended = (outs[zq] * inverse).astype(BF16)
        att_ref[zq] = attended
        delta = jnp.sum(
            own_ref[zq, 1].astype(F32) * attended.astype(F32), axis=1, keepdims=True
        )
        stat_ref[zq, 0:1] = row_of(tops[zq] + jnp.log(totals[zq]) * LOG2E)
        stat_ref[zq, 1:2] = row_of(delta)
        inverses.append(inverse)
        deltas.append(delta)
    grads = [jnp.zeros((rows, depth), F32) for _ in range(strips)]
    for zk in range(strips):
        columns = slice(zk * span, (zk + 1) * span)
        key = kv_ref[:, zk, 0].reshape(span, depth)
        value = kv_ref[:, zk, 1].reshape(span, depth)
        out_grad = own_ref[zk:, 1].reshape((strips - zk) * rows, depth)
        dots = dot_nt(out_grad, value)
        parts = []
        for zq in range(zk, strips):
            lines = slice(zq * rows, (zq + 1) * rows)
            here = dots[(zq - zk) * rows : (zq - zk + 1) * rows]
            parts.append((p_ref[lines, columns].astype(F32) * (here - deltas[zq])).astype(BF16))
        added = dot_nn(jnp.concatenate(parts, axis=0), key)
        for zq in range(zk, strips):
            grads[zq] = grads[zq] + added[(zq - zk) * rows : (zq - zk + 1) * rows]
    for zq in range(strips):
        dq_ref[zq] = (grads[zq] * (inverses[zq] * HEAD_DIM ** (-0.5))).astype(BF16)


def key_kernel(place_ref, own_ref, qd_ref, stat_ref, att_ref, dq_ref, out_ref):
    place = place_ref[0]
    ring, strips, _, rows, depth = qd_ref.shape
    span = ring * rows
    factor = HEAD_DIM ** (-0.5) * LOG2E
    line = lax.broadcasted_iota(jnp.int32, (rows, span), 0) + place * rows
    allowed = lax.broadcasted_iota(jnp.int32, (rows, span), 1) >= line
    key_sums = [jnp.zeros((rows, depth), F32) for _ in range(strips)]
    value_sums = [jnp.zeros((rows, depth), F32) for _ in range(strips)]
    for zq in range(strips):
        count = zq + 1
        query = qd_ref[:, zq, 0].reshape(span, depth)
        out_grad = qd_ref[:, zq, 1].reshape(span, depth)
        norm = jnp.concatenate([stat_ref[r, zq, 0:1] for r in range(ring)], axis=1)
        delta = jnp.concatenate([stat_ref[r, zq, 1:2] for r in range(ring)], axis=1)
        key = own_ref[:count, 0].reshape(count * rows, depth)
        value = own_ref[:count, 1].reshape(count * rows, depth)
        scores = dot_nt(key, query) * factor - norm
        last = jnp.where(allowed, scores[zq * rows :], -1e30)
        if zq:
            scores = jnp.concatenate([scores[: zq * rows], last], axis=0)
        else:
            scores = last
        weights = jnp.exp2(scores).astype(BF16)
        dots = dot_nt(value, out_grad)
        score_grad = (weights.astype(F32) * (dots - delta)).astype(BF16)
        value_added = dot_nn(weights, out_grad)
        key_added = dot_nn(score_grad, query)
        for zk in range(count):
            lines = slice(zk * rows, (zk + 1) * rows)
            value_sums[zk] = value_sums[zk] + value_added[lines]
            key_sums[zk] = key_sums[zk] + key_added[lines]
    for zk in range(strips):
        out_ref[zk, 0] = att_ref[zk]
        out_ref[zk, 1] = dq_ref[zk]
        out_ref[zk, 2] = (key_sums[zk] * HEAD_DIM ** (-0.5)).astype(BF16)
        out_ref[zk, 3] = value_sums[zk].astype(BF16)


def fill_phases(first, second, ext_ref, phase_ref):
    rows = first.shape[0]
    ext_ref[:rows] = first
    ext_ref[rows:] = second
    for r in range(8):
        phase_ref[r] = ext_ref[r : r + 2 * rows - 8]


def mix_kernel(
    left_ref, value_ref, before_ref, gate_ref, residual_ref, upstream_ref, taps_ref, skip_ref,
    gain_ref, mixed_ref, stream_ref, sums_ref, ext_ref, phase_ref,
):
    rows = left_ref.shape[0]
    taps = taps_ref.shape[0]
    product = (left_ref[...].astype(F32) * value_ref[...].astype(F32)).astype(BF16).astype(F32)
    fill_phases(before_ref[...].astype(F32), product, ext_ref, phase_ref)
    mixed = (taps_ref[0:1] + skip_ref[...]) * product
    for tap in range(1, taps):
        a, r = divmod(rows - tap, 8)
        mixed = mixed + taps_ref[tap : tap + 1] * phase_ref[r, 8 * a : 8 * a + rows]
    stream = residual_ref[...].astype(F32) + gate_ref[...].astype(F32) * mixed
    mixed_ref[...] = mixed
    stream_ref[...] = stream
    upstream = upstream_ref[...].astype(F32) * gain_ref[...]

    @pl.when(pl.program_id(0) == 0)
    def _():
        sums_ref[...] = jnp.zeros_like(sums_ref)

    sums_ref[0] += stream * stream
    sums_ref[1] += upstream * stream


def norm_kernel(
    upstream_ref, gate_ref, mixed_ref, stream_ref, gain_ref, totals_ref,
    normed_ref, residual_grad_ref, outer_grad_ref, gated_ref, gain_grad_ref, *, width,
):
    inv_rms = lax.rsqrt(totals_ref[:, 0:1] * (1.0 / width) + 1e-06)
    norm_dot = totals_ref[:, 1:2] * inv_rms * (1.0 / width)
    gain = gain_ref[...]
    upstream = upstream_ref[...].astype(F32)
    scaled = stream_ref[...] * inv_rms
    normed_ref[...] = (scaled * gain).astype(BF16)
    gain_grad_ref[...] = jnp.sum(upstream * scaled, axis=0, keepdims=True)
    stream_grad = inv_rms * (upstream * gain - scaled * norm_dot)
    residual_grad_ref[...] = stream_grad.astype(BF16)
    outer_grad_ref[...] = (stream_grad * mixed_ref[...]).astype(BF16)
    gated_ref[...] = (stream_grad * gate_ref[...].astype(F32)).astype(BF16)


def back_kernel(
    left_ref, value_ref, before_ref, gated_ref, after_ref, taps_ref, skip_ref,
    left_grad_ref, value_grad_ref, filter_ref, skip_grad_ref, ext_ref, phase_ref,
):
    rows = left_ref.shape[0]
    taps = taps_ref.shape[0]
    left = left_ref[...].astype(F32)
    value = value_ref[...].astype(F32)
    product = (left * value).astype(BF16).astype(F32)
    gated = gated_ref[...].astype(F32)
    fill_phases(gated, after_ref[...].astype(F32), ext_ref, phase_ref)
    grad = (skip_ref[...] + taps_ref[0:1]) * gated
    for tap in range(1, taps):
        a, r = divmod(tap, 8)
        grad = grad + taps_ref[tap : tap + 1] * phase_ref[r, 8 * a : 8 * a + rows]
    left_grad_ref[...] = (grad * value).astype(BF16)
    value_grad_ref[...] = (grad * left).astype(BF16)
    fill_phases(before_ref[...].astype(F32), product, ext_ref, phase_ref)
    direct = jnp.sum(gated * product, axis=0, keepdims=True)
    skip_grad_ref[...] = direct
    filter_ref[0:1] = direct
    for tap in range(1, taps):
        a, r = divmod(rows - tap, 8)
        filter_ref[tap : tap + 1] = jnp.sum(
            gated * phase_ref[r, 8 * a : 8 * a + rows], axis=0, keepdims=True
        )


def pack_kernel(*refs):
    out_ref = refs[-1]
    for h in range(out_ref.shape[0]):
        for number, ref in enumerate(refs[:-1]):
            out_ref[h, number] = ref[:, h * HEAD_DIM : (h + 1) * HEAD_DIM]


def unpack_kernel(in_ref, *refs):
    for h in range(in_ref.shape[0]):
        for number, ref in enumerate(refs):
            ref[:, h * HEAD_DIM : (h + 1) * HEAD_DIM] = in_ref[h, number]


def exchange_kernel(x_ref, out_ref, slots_ref, send_sem, recv_sem, *, team, summed):
    count = slots_ref.shape[0]
    me, device = team()
    barrier = pltpu.get_barrier_semaphore()
    for step in range(1, count):
        pl.semaphore_signal(
            barrier,
            inc=1,
            device_id=device(lax.rem(me + step, count)),
            device_id_type=pl.DeviceIdType.MESH,
        )
    slots_ref[me] = x_ref[...]
    pl.semaphore_wait(barrier, count - 1)
    copies = []
    for step in range(1, count):
        copy = pltpu.make_async_remote_copy(
            src_ref=x_ref,
            dst_ref=slots_ref.at[me],
            send_sem=send_sem.at[step - 1],
            recv_sem=recv_sem.at[step - 1],
            device_id=device(lax.rem(me + step, count)),
            device_id_type=pl.DeviceIdType.MESH,
        )
        copy.start()
        copies.append(copy)
    for copy in copies:
        copy.wait()
    if summed:
        total = slots_ref[0]
        for slot in range(1, count):
            total = total + slots_ref[slot]
        out_ref[...] = total
    else:
        out_ref[...] = slots_ref[...]


def exchange(x, count, team, summed, number, name):
    return pl.pallas_call(
        lambda *refs: exchange_kernel(*refs, team=team, summed=summed),
        in_specs=whole(1),
        out_specs=whole(1)[0],
        out_shape=shape_of(x.shape if summed else (count, *x.shape), x.dtype),
        scratch_shapes=[
            VMEM((count, *x.shape), x.dtype),
            pltpu.SemaphoreType.DMA((count - 1,)),
            pltpu.SemaphoreType.DMA((count - 1,)),
        ],
        compiler_params=pltpu.CompilerParams(collective_id=number, has_side_effects=True),
        name=name,
    )(x)


def shape_of(shape, dtype):
    return jax.ShapeDtypeStruct(shape, dtype)


def shards(
    left_stream,
    outer_gate,
    value_stream,
    residual,
    long_filter,
    skip_weight,
    norm_gain,
    normed_grad,
    attn_queries,
    attn_keys,
    attn_values,
    attended_grad,
):
    rows = left_stream.shape[1]
    channels = left_stream.shape[2]
    groups, taps = long_filter.shape
    per_group = channels // groups
    width = channels * lax.axis_size("tp")
    heads = attn_queries.shape[2] // HEAD_DIM
    devices = lax.axis_size("ctx")
    ring = devices // heads
    index = lax.axis_index("ctx")
    place = (index % ring).astype(jnp.int32).reshape(1)
    across = [[strip * ring + spot for strip in range(heads)] for spot in range(ring)]
    along = [[strip * ring + spot for spot in range(ring)] for strip in range(heads)]

    lanes = lax.axis_size("tp")
    strips = devices // ring

    def over_tp():
        return lax.axis_index("tp"), lambda peer: {"tp": peer}

    def over_ring():
        here = lax.axis_index("ctx")
        first = here // ring * ring
        return here % ring, lambda peer: {"ctx": first + peer}

    def over_strips():
        here = lax.axis_index("ctx")
        spot = here % ring
        me = lax.axis_index("dp") * strips + here // ring
        return me, lambda peer: {"dp": peer // strips, "ctx": peer % strips * ring + spot}

    stacked = pl.pallas_call(
        pack_kernel,
        in_specs=whole(4),
        out_specs=whole(1)[0],
        out_shape=shape_of((heads, 4, rows, HEAD_DIM), BF16),
        name="pack",
    )(attn_keys[0], attn_values[0], attn_queries[0], attended_grad[0])
    own = lax.all_to_all(stacked, "ctx", 0, 0, axis_index_groups=across, tiled=True)
    own_kv, own_qd = (own[:, :2], own[:, 2:])
    all_kv = lax.all_gather(own_kv, "ctx", axis=0, axis_index_groups=along, tiled=False)
    all_qd = lax.all_gather(own_qd, "ctx", axis=0, axis_index_groups=along, tiled=False)

    left, value, gate = (left_stream[0], value_stream[0], outer_gate[0])
    upstream = normed_grad[0]
    product = (left.astype(F32) * value.astype(F32)).astype(BF16)
    before = passed_along(product, "ctx", 1)
    taps_rows = jnp.repeat(long_filter.T, per_group, axis=1)
    skip, gain = (skip_weight[None, :], norm_gain[None, :])
    grid = (channels // LANES,)
    block = pl.BlockSpec((rows, LANES), lambda j: (0, j))
    tap_block = pl.BlockSpec((taps, LANES), lambda j: (0, j))
    line = pl.BlockSpec((1, LANES), lambda j: (0, j))
    phases = [VMEM((2 * rows, LANES), F32), VMEM((8, 2 * rows - 8, LANES), F32)]
    size = rows * channels
    mixed, stream, sums = pl.pallas_call(
        mix_kernel,
        grid=grid,
        in_specs=[block] * 6 + [tap_block, line, line],
        out_specs=[block, block, pl.BlockSpec((2, rows, LANES), lambda j: (0, 0, 0))],
        out_shape=[
            shape_of((rows, channels), F32),
            shape_of((rows, channels), F32),
            shape_of((2, rows, LANES), F32),
        ],
        scratch_shapes=phases,
        cost_estimate=pl.CostEstimate(
            flops=2 * taps * size, bytes_accessed=20 * size, transcendentals=0
        ),
        name="mix",
    )(left, value, before, gate, residual[0], upstream, taps_rows, skip, gain)
    totals = exchange(jnp.sum(sums, axis=2), lanes, over_tp, True, 0, "tp_sums").T
    normed, grad_residual, grad_outer, gated, gain_part = pl.pallas_call(
        lambda *refs: norm_kernel(*refs, width=width),
        in_specs=whole(6),
        out_specs=whole(5),
        out_shape=[shape_of((rows, channels), BF16)] * 4 + [shape_of((1, channels), F32)],
        cost_estimate=pl.CostEstimate(
            flops=20 * size, bytes_accessed=20 * size, transcendentals=0
        ),
        name="norm",
    )(upstream, gate, mixed, stream, gain, totals)
    after = passed_along(gated, "ctx", -1)
    grad_left, grad_value, filter_rows, skip_part = pl.pallas_call(
        back_kernel,
        grid=grid,
        in_specs=[block] * 5 + [tap_block, line],
        out_specs=[block, block, tap_block, line],
        out_shape=[
            shape_of((rows, channels), BF16),
            shape_of((rows, channels), BF16),
            shape_of((taps, channels), F32),
            shape_of((1, channels), F32),
        ],
        scratch_shapes=phases,
        cost_estimate=pl.CostEstimate(
            flops=4 * taps * size, bytes_accessed=20 * size, transcendentals=0
        ),
        name="back",
    )(left, value, before, gated, after, taps_rows, skip)
    member = (
        jnp.arange(channels, dtype=jnp.int32)[None, :] // per_group
        == jnp.arange(groups, dtype=jnp.int32)[:, None]
    ).astype(F32)
    filter_part = lax.dot_general(
        member, filter_rows, (((1,), (1,)), ((), ())), precision=lax.Precision.HIGHEST
    )
    small = jnp.concatenate(
        [filter_part.reshape(-1), skip_part.reshape(-1), gain_part.reshape(-1)]
    )
    small = exchange(small.reshape(-1, LANES), ring, over_ring, True, 1, "ring_sums")
    small = exchange(
        small, strips * lax.axis_size("dp"), over_strips, True, 2, "strip_sums"
    ).reshape(-1)
    cut = groups * taps
    filter_sum = small[:cut].reshape(groups, taps)
    skip_sum, gain_sum = (small[cut : cut + channels], small[cut + channels :])

    smem = pl.BlockSpec(memory_space=pltpu.SMEM)
    blocks = (heads, rows, HEAD_DIM)
    pairs = heads * (heads + 1) // 2 * rows * ring * rows
    attended, grad_queries, stats = pl.pallas_call(
        query_kernel,
        in_specs=[smem] + whole(2),
        out_specs=whole(3),
        out_shape=[shape_of(blocks, BF16), shape_of(blocks, BF16), shape_of((heads, 2, rows), F32)],
        scratch_shapes=[
            VMEM((heads * rows, devices * rows), F32),
            VMEM((heads * rows, devices * rows), BF16),
        ],
        cost_estimate=pl.CostEstimate(
            flops=8 * HEAD_DIM * pairs, bytes_accessed=3 << 20, transcendentals=pairs
        ),
        name="query",
    )(place, own_qd, all_kv)
    all_stats = exchange(stats, ring, over_ring, False, 3, "stats")
    back = pl.pallas_call(
        key_kernel,
        in_specs=[smem] + whole(5),
        out_specs=whole(1)[0],
        out_shape=shape_of((heads, 4, rows, HEAD_DIM), BF16),
        cost_estimate=pl.CostEstimate(
            flops=8 * HEAD_DIM * pairs, bytes_accessed=3 << 20, transcendentals=pairs
        ),
        name="key",
    )(place, own_kv, all_qd, all_stats, attended, grad_queries)
    back = lax.all_to_all(back, "ctx", 0, 0, axis_index_groups=across, tiled=True)
    back = pl.pallas_call(
        unpack_kernel,
        in_specs=whole(1),
        out_specs=whole(4),
        out_shape=[shape_of((rows, heads * HEAD_DIM), BF16)] * 4,
        name="unpack",
    )(back)
    return (
        normed[None],
        grad_left[None],
        grad_outer[None],
        grad_value[None],
        grad_residual[None],
        filter_sum,
        skip_sum,
        gain_sum,
        back[0][None],
        back[1][None],
        back[2][None],
        back[3][None],
    )


def solution(mesh):
    in_specs = (
        P("dp", "ctx", "tp"),
        P("dp", "ctx", "tp"),
        P("dp", "ctx", "tp"),
        P("dp", "ctx", "tp"),
        P("tp", None),
        P("tp"),
        P("tp"),
        P("dp", "ctx", "tp"),
        P("dp", "ctx", "tp"),
        P("dp", "ctx", "tp"),
        P("dp", "ctx", "tp"),
        P("dp", "ctx", "tp"),
    )
    out_specs = (
        P("dp", "ctx", "tp"),
        P("dp", "ctx", "tp"),
        P("dp", "ctx", "tp"),
        P("dp", "ctx", "tp"),
        P("dp", "ctx", "tp"),
        P("tp", None),
        P("tp"),
        P("tp"),
        P("dp", "ctx", "tp"),
        P("dp", "ctx", "tp"),
        P("dp", "ctx", "tp"),
        P("dp", "ctx", "tp"),
    )
    return jax.shard_map(shards, mesh=mesh, in_specs=in_specs, out_specs=out_specs, check_vma=False)
```

```python
import math

import jax
import jax.numpy as jnp
from jax import lax
from jax.experimental import pallas as pl
from jax.experimental.pallas import tpu as pltpu
from jax.sharding import PartitionSpec as P

HEAD_DIM = 128
LANES = 128
LOG2E = math.log2(math.e)
F32 = jnp.float32
BF16 = jnp.bfloat16
VMEM = pltpu.VMEM


def passed_along(value, axis, steps):
    count = lax.axis_size(axis)
    initial, last = (max(0, -steps), min(count, count - steps))
    return lax.ppermute(value, axis, [(source, source + steps) for source in range(initial, last)])


def dot_nt(a, b):
    return lax.dot_general(a, b, (((1,), (1,)), ((), ())), preferred_element_type=F32)


def dot_nn(a, b):
    return lax.dot_general(a, b, (((1,), (0,)), ((), ())), preferred_element_type=F32)


def whole(count):
    return [pl.BlockSpec(memory_space=VMEM) for _ in range(count)]


def row_of(column):
    return jnp.transpose(jnp.broadcast_to(column, (column.shape[0], LANES)))[0:1]


def query_kernel(place_ref, own_ref, kv_ref, att_ref, dq_ref, stat_ref, s_ref, p_ref):
    place = place_ref[0]
    ring, strips, _, rows, depth = kv_ref.shape
    span = ring * rows
    factor = HEAD_DIM ** (-0.5) * LOG2E
    line = lax.broadcasted_iota(jnp.int32, (rows, span), 0) + place * rows
    allowed = lax.broadcasted_iota(jnp.int32, (rows, span), 1) <= line
    tops = [None] * strips
    for zk in range(strips):
        key = kv_ref[:, zk, 0].reshape(span, depth)
        query = own_ref[zk:, 0].reshape((strips - zk) * rows, depth)
        scores = dot_nt(query, key) * factor
        for zq in range(zk, strips):
            part = scores[(zq - zk) * rows : (zq - zk + 1) * rows]
            if zq == zk:
                part = jnp.where(allowed, part, -1e30)
            s_ref[zq * rows : (zq + 1) * rows, zk * span : (zk + 1) * span] = part
            top = jnp.max(part, axis=1, keepdims=True)
            tops[zq] = top if zk == 0 else jnp.maximum(tops[zq], top)
    totals = [jnp.zeros((rows, 1), F32) for _ in range(strips)]
    outs = [jnp.zeros((rows, depth), F32) for _ in range(strips)]
    for zk in range(strips):
        columns = slice(zk * span, (zk + 1) * span)
        for zq in range(zk, strips):
            lines = slice(zq * rows, (zq + 1) * rows)
            power = jnp.exp2(s_ref[lines, columns] - tops[zq])
            totals[zq] = totals[zq] + jnp.sum(power, axis=1, keepdims=True)
            p_ref[lines, columns] = power.astype(BF16)
        value = kv_ref[:, zk, 1].reshape(span, depth)
        added = dot_nn(p_ref[zk * rows :, columns], value)
        for zq in range(zk, strips):
            outs[zq] = outs[zq] + added[(zq - zk) * rows : (zq - zk + 1) * rows]
    inverses, deltas = ([], [])
    for zq in range(strips):
        inverse = 1.0 / totals[zq]
        attended = (outs[zq] * inverse).astype(BF16)
        att_ref[zq] = attended
        delta = jnp.sum(
            own_ref[zq, 1].astype(F32) * attended.astype(F32), axis=1, keepdims=True
        )
        stat_ref[zq, 0:1] = row_of(tops[zq] + jnp.log(totals[zq]) * LOG2E)
        stat_ref[zq, 1:2] = row_of(delta)
        inverses.append(inverse)
        deltas.append(delta)
    grads = [jnp.zeros((rows, depth), F32) for _ in range(strips)]
    for zk in range(strips):
        columns = slice(zk * span, (zk + 1) * span)
        key = kv_ref[:, zk, 0].reshape(span, depth)
        value = kv_ref[:, zk, 1].reshape(span, depth)
        out_grad = own_ref[zk:, 1].reshape((strips - zk) * rows, depth)
        dots = dot_nt(out_grad, value)
        parts = []
        for zq in range(zk, strips):
            lines = slice(zq * rows, (zq + 1) * rows)
            here = dots[(zq - zk) * rows : (zq - zk + 1) * rows]
            parts.append((p_ref[lines, columns].astype(F32) * (here - deltas[zq])).astype(BF16))
        added = dot_nn(jnp.concatenate(parts, axis=0), key)
        for zq in range(zk, strips):
            grads[zq] = grads[zq] + added[(zq - zk) * rows : (zq - zk + 1) * rows]
    for zq in range(strips):
        dq_ref[zq] = (grads[zq] * (inverses[zq] * HEAD_DIM ** (-0.5))).astype(BF16)


def key_kernel(place_ref, own_ref, qd_ref, stat_ref, att_ref, dq_ref, out_ref):
    place = place_ref[0]
    ring, strips, _, rows, depth = qd_ref.shape
    span = ring * rows
    factor = HEAD_DIM ** (-0.5) * LOG2E
    line = lax.broadcasted_iota(jnp.int32, (rows, span), 0) + place * rows
    allowed = lax.broadcasted_iota(jnp.int32, (rows, span), 1) >= line
    key_sums = [jnp.zeros((rows, depth), F32) for _ in range(strips)]
    value_sums = [jnp.zeros((rows, depth), F32) for _ in range(strips)]
    for zq in range(strips):
        count = zq + 1
        query = qd_ref[:, zq, 0].reshape(span, depth)
        out_grad = qd_ref[:, zq, 1].reshape(span, depth)
        norm = jnp.concatenate([stat_ref[r, zq, 0:1] for r in range(ring)], axis=1)
        delta = jnp.concatenate([stat_ref[r, zq, 1:2] for r in range(ring)], axis=1)
        key = own_ref[:count, 0].reshape(count * rows, depth)
        value = own_ref[:count, 1].reshape(count * rows, depth)
        scores = dot_nt(key, query) * factor - norm
        last = jnp.where(allowed, scores[zq * rows :], -1e30)
        if zq:
            scores = jnp.concatenate([scores[: zq * rows], last], axis=0)
        else:
            scores = last
        weights = jnp.exp2(scores).astype(BF16)
        dots = dot_nt(value, out_grad)
        score_grad = (weights.astype(F32) * (dots - delta)).astype(BF16)
        value_added = dot_nn(weights, out_grad)
        key_added = dot_nn(score_grad, query)
        for zk in range(count):
            lines = slice(zk * rows, (zk + 1) * rows)
            value_sums[zk] = value_sums[zk] + value_added[lines]
            key_sums[zk] = key_sums[zk] + key_added[lines]
    for zk in range(strips):
        out_ref[zk, 0] = att_ref[zk]
        out_ref[zk, 1] = dq_ref[zk]
        out_ref[zk, 2] = (key_sums[zk] * HEAD_DIM ** (-0.5)).astype(BF16)
        out_ref[zk, 3] = value_sums[zk].astype(BF16)


def fill_phases(first, second, ext_ref, phase_ref):
    rows = first.shape[0]
    ext_ref[:rows] = first
    ext_ref[rows:] = second
    for r in range(8):
        phase_ref[r] = ext_ref[r : r + 2 * rows - 8]


def mix_kernel(
    left_ref, value_ref, before_ref, gate_ref, residual_ref, upstream_ref, taps_ref, skip_ref,
    gain_ref, mixed_ref, stream_ref, sums_ref, ext_ref, phase_ref,
):
    rows = left_ref.shape[0]
    taps = taps_ref.shape[0]
    product = (left_ref[...].astype(F32) * value_ref[...].astype(F32)).astype(BF16).astype(F32)
    fill_phases(before_ref[...].astype(F32), product, ext_ref, phase_ref)
    mixed = (taps_ref[0:1] + skip_ref[...]) * product
    for tap in range(1, taps):
        a, r = divmod(rows - tap, 8)
        mixed = mixed + taps_ref[tap : tap + 1] * phase_ref[r, 8 * a : 8 * a + rows]
    stream = residual_ref[...].astype(F32) + gate_ref[...].astype(F32) * mixed
    mixed_ref[...] = mixed
    stream_ref[...] = stream
    upstream = upstream_ref[...].astype(F32) * gain_ref[...]

    @pl.when(pl.program_id(0) == 0)
    def _():
        sums_ref[...] = jnp.zeros_like(sums_ref)

    sums_ref[0] += stream * stream
    sums_ref[1] += upstream * stream


def norm_kernel(
    upstream_ref, gate_ref, mixed_ref, stream_ref, gain_ref, totals_ref,
    normed_ref, residual_grad_ref, outer_grad_ref, gated_ref, gain_grad_ref, *, width,
):
    inv_rms = lax.rsqrt(totals_ref[:, 0:1] * (1.0 / width) + 1e-06)
    norm_dot = totals_ref[:, 1:2] * inv_rms * (1.0 / width)
    gain = gain_ref[...]
    upstream = upstream_ref[...].astype(F32)
    scaled = stream_ref[...] * inv_rms
    normed_ref[...] = (scaled * gain).astype(BF16)
    gain_grad_ref[...] = jnp.sum(upstream * scaled, axis=0, keepdims=True)
    stream_grad = inv_rms * (upstream * gain - scaled * norm_dot)
    residual_grad_ref[...] = stream_grad.astype(BF16)
    outer_grad_ref[...] = (stream_grad * mixed_ref[...]).astype(BF16)
    gated_ref[...] = (stream_grad * gate_ref[...].astype(F32)).astype(BF16)


def back_kernel(
    left_ref, value_ref, before_ref, gated_ref, after_ref, taps_ref, skip_ref,
    left_grad_ref, value_grad_ref, filter_ref, skip_grad_ref, ext_ref, phase_ref,
):
    rows = left_ref.shape[0]
    taps = taps_ref.shape[0]
    left = left_ref[...].astype(F32)
    value = value_ref[...].astype(F32)
    product = (left * value).astype(BF16).astype(F32)
    gated = gated_ref[...].astype(F32)
    fill_phases(gated, after_ref[...].astype(F32), ext_ref, phase_ref)
    grad = (skip_ref[...] + taps_ref[0:1]) * gated
    for tap in range(1, taps):
        a, r = divmod(tap, 8)
        grad = grad + taps_ref[tap : tap + 1] * phase_ref[r, 8 * a : 8 * a + rows]
    left_grad_ref[...] = (grad * value).astype(BF16)
    value_grad_ref[...] = (grad * left).astype(BF16)
    fill_phases(before_ref[...].astype(F32), product, ext_ref, phase_ref)
    direct = jnp.sum(gated * product, axis=0, keepdims=True)
    skip_grad_ref[...] = direct
    filter_ref[0:1] = direct
    for tap in range(1, taps):
        a, r = divmod(rows - tap, 8)
        filter_ref[tap : tap + 1] = jnp.sum(
            gated * phase_ref[r, 8 * a : 8 * a + rows], axis=0, keepdims=True
        )


def pack_kernel(key_ref, value_ref, query_ref, grad_ref, kv_ref, qd_ref):
    for h in range(kv_ref.shape[0]):
        columns = slice(h * HEAD_DIM, (h + 1) * HEAD_DIM)
        kv_ref[h, 0] = key_ref[:, columns]
        kv_ref[h, 1] = value_ref[:, columns]
        qd_ref[h, 0] = query_ref[:, columns]
        qd_ref[h, 1] = grad_ref[:, columns]


def unpack_kernel(in_ref, *refs):
    for h in range(in_ref.shape[0]):
        for number, ref in enumerate(refs):
            ref[:, h * HEAD_DIM : (h + 1) * HEAD_DIM] = in_ref[h, number]


def exchange_kernel(x_ref, out_ref, slots_ref, send_sem, recv_sem, *, team, summed):
    count = slots_ref.shape[0]
    me, device = team()
    barrier = pltpu.get_barrier_semaphore()
    for step in range(1, count):
        pl.semaphore_signal(
            barrier,
            inc=1,
            device_id=device(lax.rem(me + step, count)),
            device_id_type=pl.DeviceIdType.MESH,
        )
    slots_ref[me] = x_ref[...]
    pl.semaphore_wait(barrier, count - 1)
    copies = []
    for step in range(1, count):
        copy = pltpu.make_async_remote_copy(
            src_ref=x_ref,
            dst_ref=slots_ref.at[me],
            send_sem=send_sem.at[step - 1],
            recv_sem=recv_sem.at[step - 1],
            device_id=device(lax.rem(me + step, count)),
            device_id_type=pl.DeviceIdType.MESH,
        )
        copy.start()
        copies.append(copy)
    for copy in copies:
        copy.wait()
    if summed:
        total = slots_ref[0]
        for slot in range(1, count):
            total = total + slots_ref[slot]
        out_ref[...] = total
    else:
        out_ref[...] = slots_ref[...]


def exchange(x, count, team, summed, number, name):
    return pl.pallas_call(
        lambda *refs: exchange_kernel(*refs, team=team, summed=summed),
        in_specs=whole(1),
        out_specs=whole(1)[0],
        out_shape=shape_of(x.shape if summed else (count, *x.shape), x.dtype),
        scratch_shapes=[
            VMEM((count, *x.shape), x.dtype),
            pltpu.SemaphoreType.DMA((count - 1,)),
            pltpu.SemaphoreType.DMA((count - 1,)),
        ],
        compiler_params=pltpu.CompilerParams(collective_id=number, has_side_effects=True),
        name=name,
    )(x)


def shape_of(shape, dtype):
    return jax.ShapeDtypeStruct(shape, dtype)


def shards(
    left_stream,
    outer_gate,
    value_stream,
    residual,
    long_filter,
    skip_weight,
    norm_gain,
    normed_grad,
    attn_queries,
    attn_keys,
    attn_values,
    attended_grad,
):
    rows = left_stream.shape[1]
    channels = left_stream.shape[2]
    groups, taps = long_filter.shape
    per_group = channels // groups
    width = channels * lax.axis_size("tp")
    heads = attn_queries.shape[2] // HEAD_DIM
    devices = lax.axis_size("ctx")
    ring = devices // heads
    index = lax.axis_index("ctx")
    place = (index % ring).astype(jnp.int32).reshape(1)
    across = [[strip * ring + spot for strip in range(heads)] for spot in range(ring)]
    along = [[strip * ring + spot for spot in range(ring)] for strip in range(heads)]

    lanes = lax.axis_size("tp")
    strips = devices // ring

    def over_tp():
        return lax.axis_index("tp"), lambda peer: {"tp": peer}

    def over_ring():
        here = lax.axis_index("ctx")
        first = here // ring * ring
        return here % ring, lambda peer: {"ctx": first + peer}

    def over_strips():
        here = lax.axis_index("ctx")
        spot = here % ring
        me = lax.axis_index("dp") * strips + here // ring
        return me, lambda peer: {"dp": peer // strips, "ctx": peer % strips * ring + spot}

    pair = shape_of((heads, 2, rows, HEAD_DIM), BF16)
    send_kv, send_qd = pl.pallas_call(
        pack_kernel,
        in_specs=whole(4),
        out_specs=whole(2),
        out_shape=[pair, pair],
        name="pack",
    )(attn_keys[0], attn_values[0], attn_queries[0], attended_grad[0])
    own_kv = lax.all_to_all(send_kv, "ctx", 0, 0, axis_index_groups=across, tiled=True)
    all_kv = lax.all_gather(own_kv, "ctx", axis=0, axis_index_groups=along, tiled=False)
    own_kv, send_qd = lax.optimization_barrier((own_kv, send_qd))
    own_qd = lax.all_to_all(send_qd, "ctx", 0, 0, axis_index_groups=across, tiled=True)
    all_qd = lax.all_gather(own_qd, "ctx", axis=0, axis_index_groups=along, tiled=False)

    own_qd, left_stream = lax.optimization_barrier((own_qd, left_stream))
    left, value, gate = (left_stream[0], value_stream[0], outer_gate[0])
    upstream = normed_grad[0]
    product = (left.astype(F32) * value.astype(F32)).astype(BF16)
    before = passed_along(product, "ctx", 1)
    taps_rows = jnp.repeat(long_filter.T, per_group, axis=1)
    skip, gain = (skip_weight[None, :], norm_gain[None, :])
    grid = (channels // LANES,)
    block = pl.BlockSpec((rows, LANES), lambda j: (0, j))
    tap_block = pl.BlockSpec((taps, LANES), lambda j: (0, j))
    line = pl.BlockSpec((1, LANES), lambda j: (0, j))
    phases = [VMEM((2 * rows, LANES), F32), VMEM((8, 2 * rows - 8, LANES), F32)]
    size = rows * channels
    mixed, stream, sums = pl.pallas_call(
        mix_kernel,
        grid=grid,
        in_specs=[block] * 6 + [tap_block, line, line],
        out_specs=[block, block, pl.BlockSpec((2, rows, LANES), lambda j: (0, 0, 0))],
        out_shape=[
            shape_of((rows, channels), F32),
            shape_of((rows, channels), F32),
            shape_of((2, rows, LANES), F32),
        ],
        scratch_shapes=phases,
        cost_estimate=pl.CostEstimate(
            flops=2 * taps * size, bytes_accessed=20 * size, transcendentals=0
        ),
        name="mix",
    )(left, value, before, gate, residual[0], upstream, taps_rows, skip, gain)
    totals = exchange(jnp.sum(sums, axis=2), lanes, over_tp, True, 0, "tp_sums").T
    normed, grad_residual, grad_outer, gated, gain_part = pl.pallas_call(
        lambda *refs: norm_kernel(*refs, width=width),
        in_specs=whole(6),
        out_specs=whole(5),
        out_shape=[shape_of((rows, channels), BF16)] * 4 + [shape_of((1, channels), F32)],
        cost_estimate=pl.CostEstimate(
            flops=20 * size, bytes_accessed=20 * size, transcendentals=0
        ),
        name="norm",
    )(upstream, gate, mixed, stream, gain, totals)
    after = passed_along(gated, "ctx", -1)
    grad_left, grad_value, filter_rows, skip_part = pl.pallas_call(
        back_kernel,
        grid=grid,
        in_specs=[block] * 5 + [tap_block, line],
        out_specs=[block, block, tap_block, line],
        out_shape=[
            shape_of((rows, channels), BF16),
            shape_of((rows, channels), BF16),
            shape_of((taps, channels), F32),
            shape_of((1, channels), F32),
        ],
        scratch_shapes=phases,
        cost_estimate=pl.CostEstimate(
            flops=4 * taps * size, bytes_accessed=20 * size, transcendentals=0
        ),
        name="back",
    )(left, value, before, gated, after, taps_rows, skip)
    member = (
        jnp.arange(channels, dtype=jnp.int32)[None, :] // per_group
        == jnp.arange(groups, dtype=jnp.int32)[:, None]
    ).astype(F32)
    filter_part = lax.dot_general(
        member, filter_rows, (((1,), (1,)), ((), ())), precision=lax.Precision.HIGHEST
    )
    small = jnp.concatenate(
        [filter_part.reshape(-1), skip_part.reshape(-1), gain_part.reshape(-1)]
    )
    small, own_qd = lax.optimization_barrier((small.reshape(-1, LANES), own_qd))
    small = exchange(small, ring, over_ring, True, 1, "ring_sums")
    small = exchange(
        small, strips * lax.axis_size("dp"), over_strips, True, 2, "strip_sums"
    ).reshape(-1)
    small, own_kv = lax.optimization_barrier((small, own_kv))
    cut = groups * taps
    filter_sum = small[:cut].reshape(groups, taps)
    skip_sum, gain_sum = (small[cut : cut + channels], small[cut + channels :])

    smem = pl.BlockSpec(memory_space=pltpu.SMEM)
    blocks = (heads, rows, HEAD_DIM)
    pairs = heads * (heads + 1) // 2 * rows * ring * rows
    attended, grad_queries, stats = pl.pallas_call(
        query_kernel,
        in_specs=[smem] + whole(2),
        out_specs=whole(3),
        out_shape=[shape_of(blocks, BF16), shape_of(blocks, BF16), shape_of((heads, 2, rows), F32)],
        scratch_shapes=[
            VMEM((heads * rows, devices * rows), F32),
            VMEM((heads * rows, devices * rows), BF16),
        ],
        cost_estimate=pl.CostEstimate(
            flops=8 * HEAD_DIM * pairs, bytes_accessed=3 << 20, transcendentals=pairs
        ),
        name="query",
    )(place, own_qd, all_kv)
    all_stats = exchange(stats, ring, over_ring, False, 3, "stats")
    back = pl.pallas_call(
        key_kernel,
        in_specs=[smem] + whole(5),
        out_specs=whole(1)[0],
        out_shape=shape_of((heads, 4, rows, HEAD_DIM), BF16),
        cost_estimate=pl.CostEstimate(
            flops=8 * HEAD_DIM * pairs, bytes_accessed=3 << 20, transcendentals=pairs
        ),
        name="key",
    )(place, own_kv, all_qd, all_stats, attended, grad_queries)
    back = lax.all_to_all(back, "ctx", 0, 0, axis_index_groups=across, tiled=True)
    back = pl.pallas_call(
        unpack_kernel,
        in_specs=whole(1),
        out_specs=whole(4),
        out_shape=[shape_of((rows, heads * HEAD_DIM), BF16)] * 4,
        name="unpack",
    )(back)
    return (
        normed[None],
        grad_left[None],
        grad_outer[None],
        grad_value[None],
        grad_residual[None],
        filter_sum,
        skip_sum,
        gain_sum,
        back[0][None],
        back[1][None],
        back[2][None],
        back[3][None],
    )


def solution(mesh):
    in_specs = (
        P("dp", "ctx", "tp"),
        P("dp", "ctx", "tp"),
        P("dp", "ctx", "tp"),
        P("dp", "ctx", "tp"),
        P("tp", None),
        P("tp"),
        P("tp"),
        P("dp", "ctx", "tp"),
        P("dp", "ctx", "tp"),
        P("dp", "ctx", "tp"),
        P("dp", "ctx", "tp"),
        P("dp", "ctx", "tp"),
    )
    out_specs = (
        P("dp", "ctx", "tp"),
        P("dp", "ctx", "tp"),
        P("dp", "ctx", "tp"),
        P("dp", "ctx", "tp"),
        P("dp", "ctx", "tp"),
        P("tp", None),
        P("tp"),
        P("tp"),
        P("dp", "ctx", "tp"),
        P("dp", "ctx", "tp"),
        P("dp", "ctx", "tp"),
        P("dp", "ctx", "tp"),
    )
    return jax.shard_map(shards, mesh=mesh, in_specs=in_specs, out_specs=out_specs, check_vma=False)
```

```python
import math

import jax
import jax.numpy as jnp
from jax import lax
from jax.experimental import pallas as pl
from jax.experimental.pallas import tpu as pltpu
from jax.sharding import PartitionSpec as P

HEAD_DIM = 128
LANES = 128
LOG2E = math.log2(math.e)
F32 = jnp.float32
BF16 = jnp.bfloat16
VMEM = pltpu.VMEM


def passed_along(value, axis, steps):
    count = lax.axis_size(axis)
    initial, last = (max(0, -steps), min(count, count - steps))
    return lax.ppermute(value, axis, [(source, source + steps) for source in range(initial, last)])


def dot_nt(a, b):
    return lax.dot_general(a, b, (((1,), (1,)), ((), ())), preferred_element_type=F32)


def dot_nn(a, b):
    return lax.dot_general(a, b, (((1,), (0,)), ((), ())), preferred_element_type=F32)


def whole(count):
    return [pl.BlockSpec(memory_space=VMEM) for _ in range(count)]


def row_of(column):
    return jnp.transpose(jnp.broadcast_to(column, (column.shape[0], LANES)))[0:1]


def query_kernel(place_ref, own_ref, kv_ref, att_ref, dq_ref, stat_ref, s_ref, p_ref):
    place = place_ref[0]
    ring, strips, _, rows, depth = kv_ref.shape
    span = ring * rows
    factor = HEAD_DIM ** (-0.5) * LOG2E
    line = lax.broadcasted_iota(jnp.int32, (rows, span), 0) + place * rows
    allowed = lax.broadcasted_iota(jnp.int32, (rows, span), 1) <= line
    tops = [None] * strips
    for zk in range(strips):
        key = kv_ref[:, zk, 0].reshape(span, depth)
        query = own_ref[zk:, 0].reshape((strips - zk) * rows, depth)
        scores = dot_nt(query, key) * factor
        for zq in range(zk, strips):
            part = scores[(zq - zk) * rows : (zq - zk + 1) * rows]
            if zq == zk:
                part = jnp.where(allowed, part, -1e30)
            s_ref[zq * rows : (zq + 1) * rows, zk * span : (zk + 1) * span] = part
            top = jnp.max(part, axis=1, keepdims=True)
            tops[zq] = top if zk == 0 else jnp.maximum(tops[zq], top)
    totals = [jnp.zeros((rows, 1), F32) for _ in range(strips)]
    outs = [jnp.zeros((rows, depth), F32) for _ in range(strips)]
    for zk in range(strips):
        columns = slice(zk * span, (zk + 1) * span)
        for zq in range(zk, strips):
            lines = slice(zq * rows, (zq + 1) * rows)
            power = jnp.exp2(s_ref[lines, columns] - tops[zq])
            totals[zq] = totals[zq] + jnp.sum(power, axis=1, keepdims=True)
            p_ref[lines, columns] = power.astype(BF16)
        value = kv_ref[:, zk, 1].reshape(span, depth)
        added = dot_nn(p_ref[zk * rows :, columns], value)
        for zq in range(zk, strips):
            outs[zq] = outs[zq] + added[(zq - zk) * rows : (zq - zk + 1) * rows]
    inverses, deltas = ([], [])
    for zq in range(strips):
        inverse = 1.0 / totals[zq]
        attended = (outs[zq] * inverse).astype(BF16)
        att_ref[zq] = attended
        delta = jnp.sum(
            own_ref[zq, 1].astype(F32) * attended.astype(F32), axis=1, keepdims=True
        )
        stat_ref[zq, 0:1] = row_of(tops[zq] + jnp.log(totals[zq]) * LOG2E)
        stat_ref[zq, 1:2] = row_of(delta)
        inverses.append(inverse)
        deltas.append(delta)
    grads = [jnp.zeros((rows, depth), F32) for _ in range(strips)]
    for zk in range(strips):
        columns = slice(zk * span, (zk + 1) * span)
        key = kv_ref[:, zk, 0].reshape(span, depth)
        value = kv_ref[:, zk, 1].reshape(span, depth)
        out_grad = own_ref[zk:, 1].reshape((strips - zk) * rows, depth)
        dots = dot_nt(out_grad, value)
        parts = []
        for zq in range(zk, strips):
            lines = slice(zq * rows, (zq + 1) * rows)
            here = dots[(zq - zk) * rows : (zq - zk + 1) * rows]
            parts.append((p_ref[lines, columns].astype(F32) * (here - deltas[zq])).astype(BF16))
        added = dot_nn(jnp.concatenate(parts, axis=0), key)
        for zq in range(zk, strips):
            grads[zq] = grads[zq] + added[(zq - zk) * rows : (zq - zk + 1) * rows]
    for zq in range(strips):
        dq_ref[zq] = (grads[zq] * (inverses[zq] * HEAD_DIM ** (-0.5))).astype(BF16)


def key_kernel(place_ref, own_ref, stat_ref, att_ref, dq_ref, *refs):
    *hop_refs, out_ref, qd_ref = refs
    place = place_ref[0]
    for step, hop_ref in enumerate(hop_refs):
        qd_ref[lax.rem(place - step + len(hop_refs), len(hop_refs))] = hop_ref[...]
    ring, strips, _, rows, depth = qd_ref.shape
    span = ring * rows
    factor = HEAD_DIM ** (-0.5) * LOG2E
    line = lax.broadcasted_iota(jnp.int32, (rows, span), 0) + place * rows
    allowed = lax.broadcasted_iota(jnp.int32, (rows, span), 1) >= line
    key_sums = [jnp.zeros((rows, depth), F32) for _ in range(strips)]
    value_sums = [jnp.zeros((rows, depth), F32) for _ in range(strips)]
    for zq in range(strips):
        count = zq + 1
        query = qd_ref[:, zq, 0].reshape(span, depth)
        out_grad = qd_ref[:, zq, 1].reshape(span, depth)
        norm = jnp.concatenate([stat_ref[r, zq, 0:1] for r in range(ring)], axis=1)
        delta = jnp.concatenate([stat_ref[r, zq, 1:2] for r in range(ring)], axis=1)
        key = own_ref[:count, 0].reshape(count * rows, depth)
        value = own_ref[:count, 1].reshape(count * rows, depth)
        scores = dot_nt(key, query) * factor - norm
        last = jnp.where(allowed, scores[zq * rows :], -1e30)
        if zq:
            scores = jnp.concatenate([scores[: zq * rows], last], axis=0)
        else:
            scores = last
        weights = jnp.exp2(scores).astype(BF16)
        dots = dot_nt(value, out_grad)
        score_grad = (weights.astype(F32) * (dots - delta)).astype(BF16)
        value_added = dot_nn(weights, out_grad)
        key_added = dot_nn(score_grad, query)
        for zk in range(count):
            lines = slice(zk * rows, (zk + 1) * rows)
            value_sums[zk] = value_sums[zk] + value_added[lines]
            key_sums[zk] = key_sums[zk] + key_added[lines]
    for zk in range(strips):
        out_ref[zk, 0] = att_ref[zk]
        out_ref[zk, 1] = dq_ref[zk]
        out_ref[zk, 2] = (key_sums[zk] * HEAD_DIM ** (-0.5)).astype(BF16)
        out_ref[zk, 3] = value_sums[zk].astype(BF16)


def fill_phases(first, second, ext_ref, phase_ref):
    rows = first.shape[0]
    ext_ref[:rows] = first
    ext_ref[rows:] = second
    for r in range(8):
        phase_ref[r] = ext_ref[r : r + 2 * rows - 8]


def mix_kernel(
    left_ref, value_ref, before_ref, gate_ref, residual_ref, upstream_ref, taps_ref, skip_ref,
    gain_ref, mixed_ref, stream_ref, sums_ref, ext_ref, phase_ref,
):
    rows = left_ref.shape[0]
    taps = taps_ref.shape[0]
    product = (left_ref[...].astype(F32) * value_ref[...].astype(F32)).astype(BF16).astype(F32)
    fill_phases(before_ref[...].astype(F32), product, ext_ref, phase_ref)
    mixed = (taps_ref[0:1] + skip_ref[...]) * product
    for tap in range(1, taps):
        a, r = divmod(rows - tap, 8)
        mixed = mixed + taps_ref[tap : tap + 1] * phase_ref[r, 8 * a : 8 * a + rows]
    stream = residual_ref[...].astype(F32) + gate_ref[...].astype(F32) * mixed
    mixed_ref[...] = mixed
    stream_ref[...] = stream
    upstream = upstream_ref[...].astype(F32) * gain_ref[...]

    @pl.when(pl.program_id(0) == 0)
    def _():
        sums_ref[...] = jnp.zeros_like(sums_ref)

    sums_ref[0] += stream * stream
    sums_ref[1] += upstream * stream


def norm_kernel(
    upstream_ref, gate_ref, mixed_ref, stream_ref, gain_ref, totals_ref,
    normed_ref, residual_grad_ref, outer_grad_ref, gated_ref, gain_grad_ref, *, width,
):
    inv_rms = lax.rsqrt(totals_ref[:, 0:1] * (1.0 / width) + 1e-06)
    norm_dot = totals_ref[:, 1:2] * inv_rms * (1.0 / width)
    gain = gain_ref[...]
    upstream = upstream_ref[...].astype(F32)
    scaled = stream_ref[...] * inv_rms
    normed_ref[...] = (scaled * gain).astype(BF16)
    gain_grad_ref[...] = jnp.sum(upstream * scaled, axis=0, keepdims=True)
    stream_grad = inv_rms * (upstream * gain - scaled * norm_dot)
    residual_grad_ref[...] = stream_grad.astype(BF16)
    outer_grad_ref[...] = (stream_grad * mixed_ref[...]).astype(BF16)
    gated_ref[...] = (stream_grad * gate_ref[...].astype(F32)).astype(BF16)


def back_kernel(
    left_ref, value_ref, before_ref, gated_ref, after_ref, taps_ref, skip_ref,
    left_grad_ref, value_grad_ref, filter_ref, skip_grad_ref, ext_ref, phase_ref,
):
    rows = left_ref.shape[0]
    taps = taps_ref.shape[0]
    left = left_ref[...].astype(F32)
    value = value_ref[...].astype(F32)
    product = (left * value).astype(BF16).astype(F32)
    gated = gated_ref[...].astype(F32)
    fill_phases(gated, after_ref[...].astype(F32), ext_ref, phase_ref)
    grad = (skip_ref[...] + taps_ref[0:1]) * gated
    for tap in range(1, taps):
        a, r = divmod(tap, 8)
        grad = grad + taps_ref[tap : tap + 1] * phase_ref[r, 8 * a : 8 * a + rows]
    left_grad_ref[...] = (grad * value).astype(BF16)
    value_grad_ref[...] = (grad * left).astype(BF16)
    fill_phases(before_ref[...].astype(F32), product, ext_ref, phase_ref)
    direct = jnp.sum(gated * product, axis=0, keepdims=True)
    skip_grad_ref[...] = direct
    filter_ref[0:1] = direct
    for tap in range(1, taps):
        a, r = divmod(rows - tap, 8)
        filter_ref[tap : tap + 1] = jnp.sum(
            gated * phase_ref[r, 8 * a : 8 * a + rows], axis=0, keepdims=True
        )


def pack_kernel(key_ref, value_ref, query_ref, grad_ref, kv_ref, qd_ref):
    for h in range(kv_ref.shape[0]):
        columns = slice(h * HEAD_DIM, (h + 1) * HEAD_DIM)
        kv_ref[h, 0] = key_ref[:, columns]
        kv_ref[h, 1] = value_ref[:, columns]
        qd_ref[h, 0] = query_ref[:, columns]
        qd_ref[h, 1] = grad_ref[:, columns]


def unpack_kernel(in_ref, *refs):
    for h in range(in_ref.shape[0]):
        for number, ref in enumerate(refs):
            ref[:, h * HEAD_DIM : (h + 1) * HEAD_DIM] = in_ref[h, number]


def exchange_kernel(x_ref, out_ref, slots_ref, send_sem, recv_sem, *, team, summed):
    count = slots_ref.shape[0]
    me, device = team()
    barrier = pltpu.get_barrier_semaphore()
    for step in range(1, count):
        pl.semaphore_signal(
            barrier,
            inc=1,
            device_id=device(lax.rem(me + step, count)),
            device_id_type=pl.DeviceIdType.MESH,
        )
    slots_ref[me] = x_ref[...]
    pl.semaphore_wait(barrier, count - 1)
    copies = []
    for step in range(1, count):
        copy = pltpu.make_async_remote_copy(
            src_ref=x_ref,
            dst_ref=slots_ref.at[me],
            send_sem=send_sem.at[step - 1],
            recv_sem=recv_sem.at[step - 1],
            device_id=device(lax.rem(me + step, count)),
            device_id_type=pl.DeviceIdType.MESH,
        )
        copy.start()
        copies.append(copy)
    for copy in copies:
        copy.wait()
    if summed:
        total = slots_ref[0]
        for slot in range(1, count):
            total = total + slots_ref[slot]
        out_ref[...] = total
    else:
        out_ref[...] = slots_ref[...]


def exchange(x, count, team, summed, number, name):
    return pl.pallas_call(
        lambda *refs: exchange_kernel(*refs, team=team, summed=summed),
        in_specs=whole(1),
        out_specs=whole(1)[0],
        out_shape=shape_of(x.shape if summed else (count, *x.shape), x.dtype),
        scratch_shapes=[
            VMEM((count, *x.shape), x.dtype),
            pltpu.SemaphoreType.DMA((count - 1,)),
            pltpu.SemaphoreType.DMA((count - 1,)),
        ],
        compiler_params=pltpu.CompilerParams(collective_id=number, has_side_effects=True),
        name=name,
    )(x)


def shape_of(shape, dtype):
    return jax.ShapeDtypeStruct(shape, dtype)


def shards(
    left_stream,
    outer_gate,
    value_stream,
    residual,
    long_filter,
    skip_weight,
    norm_gain,
    normed_grad,
    attn_queries,
    attn_keys,
    attn_values,
    attended_grad,
):
    rows = left_stream.shape[1]
    channels = left_stream.shape[2]
    groups, taps = long_filter.shape
    per_group = channels // groups
    width = channels * lax.axis_size("tp")
    heads = attn_queries.shape[2] // HEAD_DIM
    devices = lax.axis_size("ctx")
    ring = devices // heads
    index = lax.axis_index("ctx")
    place = (index % ring).astype(jnp.int32).reshape(1)
    across = [[strip * ring + spot for strip in range(heads)] for spot in range(ring)]
    along = [[strip * ring + spot for spot in range(ring)] for strip in range(heads)]

    lanes = lax.axis_size("tp")
    strips = devices // ring

    def over_tp():
        return lax.axis_index("tp"), lambda peer: {"tp": peer}

    def over_ring():
        here = lax.axis_index("ctx")
        first = here // ring * ring
        return here % ring, lambda peer: {"ctx": first + peer}

    def over_strips():
        here = lax.axis_index("ctx")
        spot = here % ring
        me = lax.axis_index("dp") * strips + here // ring
        return me, lambda peer: {"dp": peer // strips, "ctx": peer % strips * ring + spot}

    pair = shape_of((heads, 2, rows, HEAD_DIM), BF16)
    send_kv, send_qd = pl.pallas_call(
        pack_kernel,
        in_specs=whole(4),
        out_specs=whole(2),
        out_shape=[pair, pair],
        name="pack",
    )(attn_keys[0], attn_values[0], attn_queries[0], attended_grad[0])
    own_kv = lax.all_to_all(send_kv, "ctx", 0, 0, axis_index_groups=across, tiled=True)
    all_kv = lax.all_gather(own_kv, "ctx", axis=0, axis_index_groups=along, tiled=False)
    own_kv, send_qd = lax.optimization_barrier((own_kv, send_qd))
    own_qd = lax.all_to_all(send_qd, "ctx", 0, 0, axis_index_groups=across, tiled=True)
    hops = [own_qd]
    for step in range(1, ring):
        pairs = [
            (team[spot], team[(spot + step) % ring]) for team in along for spot in range(ring)
        ]
        hops.append(lax.ppermute(own_qd, "ctx", pairs))

    own_qd, left_stream = lax.optimization_barrier((own_qd, left_stream))
    left, value, gate = (left_stream[0], value_stream[0], outer_gate[0])
    upstream = normed_grad[0]
    product = (left.astype(F32) * value.astype(F32)).astype(BF16)
    before = passed_along(product, "ctx", 1)
    taps_rows = jnp.repeat(long_filter.T, per_group, axis=1)
    skip, gain = (skip_weight[None, :], norm_gain[None, :])
    grid = (channels // LANES,)
    block = pl.BlockSpec((rows, LANES), lambda j: (0, j))
    tap_block = pl.BlockSpec((taps, LANES), lambda j: (0, j))
    line = pl.BlockSpec((1, LANES), lambda j: (0, j))
    phases = [VMEM((2 * rows, LANES), F32), VMEM((8, 2 * rows - 8, LANES), F32)]
    size = rows * channels
    mixed, stream, sums = pl.pallas_call(
        mix_kernel,
        grid=grid,
        in_specs=[block] * 6 + [tap_block, line, line],
        out_specs=[block, block, pl.BlockSpec((2, rows, LANES), lambda j: (0, 0, 0))],
        out_shape=[
            shape_of((rows, channels), F32),
            shape_of((rows, channels), F32),
            shape_of((2, rows, LANES), F32),
        ],
        scratch_shapes=phases,
        cost_estimate=pl.CostEstimate(
            flops=2 * taps * size, bytes_accessed=20 * size, transcendentals=0
        ),
        name="mix",
    )(left, value, before, gate, residual[0], upstream, taps_rows, skip, gain)
    totals = exchange(jnp.sum(sums, axis=2), lanes, over_tp, True, 0, "tp_sums").T
    normed, grad_residual, grad_outer, gated, gain_part = pl.pallas_call(
        lambda *refs: norm_kernel(*refs, width=width),
        in_specs=whole(6),
        out_specs=whole(5),
        out_shape=[shape_of((rows, channels), BF16)] * 4 + [shape_of((1, channels), F32)],
        cost_estimate=pl.CostEstimate(
            flops=20 * size, bytes_accessed=20 * size, transcendentals=0
        ),
        name="norm",
    )(upstream, gate, mixed, stream, gain, totals)
    after = passed_along(gated, "ctx", -1)
    grad_left, grad_value, filter_rows, skip_part = pl.pallas_call(
        back_kernel,
        grid=grid,
        in_specs=[block] * 5 + [tap_block, line],
        out_specs=[block, block, tap_block, line],
        out_shape=[
            shape_of((rows, channels), BF16),
            shape_of((rows, channels), BF16),
            shape_of((taps, channels), F32),
            shape_of((1, channels), F32),
        ],
        scratch_shapes=phases,
        cost_estimate=pl.CostEstimate(
            flops=4 * taps * size, bytes_accessed=20 * size, transcendentals=0
        ),
        name="back",
    )(left, value, before, gated, after, taps_rows, skip)
    member = (
        jnp.arange(channels, dtype=jnp.int32)[None, :] // per_group
        == jnp.arange(groups, dtype=jnp.int32)[:, None]
    ).astype(F32)
    filter_part = lax.dot_general(
        member, filter_rows, (((1,), (1,)), ((), ())), precision=lax.Precision.HIGHEST
    )
    small = jnp.concatenate(
        [filter_part.reshape(-1), skip_part.reshape(-1), gain_part.reshape(-1)]
    )
    small, own_qd = lax.optimization_barrier((small.reshape(-1, LANES), own_qd))

    smem = pl.BlockSpec(memory_space=pltpu.SMEM)
    blocks = (heads, rows, HEAD_DIM)
    pairs = heads * (heads + 1) // 2 * rows * ring * rows
    attended, grad_queries, stats = pl.pallas_call(
        query_kernel,
        in_specs=[smem] + whole(2),
        out_specs=whole(3),
        out_shape=[shape_of(blocks, BF16), shape_of(blocks, BF16), shape_of((heads, 2, rows), F32)],
        scratch_shapes=[
            VMEM((heads * rows, devices * rows), F32),
            VMEM((heads * rows, devices * rows), BF16),
        ],
        cost_estimate=pl.CostEstimate(
            flops=8 * HEAD_DIM * pairs, bytes_accessed=3 << 20, transcendentals=pairs
        ),
        name="query",
    )(place, own_qd, all_kv)
    lines = 2 * heads
    gathered = exchange(
        jnp.concatenate([stats.reshape(lines, rows), small], axis=0),
        ring, over_ring, False, 1, "ring_gather",
    )
    all_stats = gathered[:, :lines].reshape(ring, heads, 2, rows)
    back = pl.pallas_call(
        key_kernel,
        in_specs=[smem] + whole(4 + ring),
        out_specs=whole(1)[0],
        out_shape=shape_of((heads, 4, rows, HEAD_DIM), BF16),
        scratch_shapes=[VMEM((ring, heads, 2, rows, HEAD_DIM), BF16)],
        cost_estimate=pl.CostEstimate(
            flops=8 * HEAD_DIM * pairs, bytes_accessed=3 << 20, transcendentals=pairs
        ),
        name="key",
    )(place, own_kv, all_stats, attended, grad_queries, *hops)
    back, gathered = lax.optimization_barrier((back, gathered))
    back = lax.all_to_all(back, "ctx", 0, 0, axis_index_groups=across, tiled=True)
    back = pl.pallas_call(
        unpack_kernel,
        in_specs=whole(1),
        out_specs=whole(4),
        out_shape=[shape_of((rows, heads * HEAD_DIM), BF16)] * 4,
        name="unpack",
    )(back)
    small = exchange(
        jnp.sum(gathered[:, lines:], axis=0),
        strips * lax.axis_size("dp"), over_strips, True, 2, "strip_sums",
    ).reshape(-1)
    cut = groups * taps
    filter_sum = small[:cut].reshape(groups, taps)
    skip_sum, gain_sum = (small[cut : cut + channels], small[cut + channels :])
    return (
        normed[None],
        grad_left[None],
        grad_outer[None],
        grad_value[None],
        grad_residual[None],
        filter_sum,
        skip_sum,
        gain_sum,
        back[0][None],
        back[1][None],
        back[2][None],
        back[3][None],
    )


def solution(mesh):
    in_specs = (
        P("dp", "ctx", "tp"),
        P("dp", "ctx", "tp"),
        P("dp", "ctx", "tp"),
        P("dp", "ctx", "tp"),
        P("tp", None),
        P("tp"),
        P("tp"),
        P("dp", "ctx", "tp"),
        P("dp", "ctx", "tp"),
        P("dp", "ctx", "tp"),
        P("dp", "ctx", "tp"),
        P("dp", "ctx", "tp"),
    )
    out_specs = (
        P("dp", "ctx", "tp"),
        P("dp", "ctx", "tp"),
        P("dp", "ctx", "tp"),
        P("dp", "ctx", "tp"),
        P("dp", "ctx", "tp"),
        P("tp", None),
        P("tp"),
        P("tp"),
        P("dp", "ctx", "tp"),
        P("dp", "ctx", "tp"),
        P("dp", "ctx", "tp"),
        P("dp", "ctx", "tp"),
    )
    return jax.shard_map(shards, mesh=mesh, in_specs=in_specs, out_specs=out_specs, check_vma=False)
```

```python
import math

import jax
import jax.numpy as jnp
from jax import lax
from jax.experimental import pallas as pl
from jax.experimental.pallas import tpu as pltpu
from jax.sharding import PartitionSpec as P

HEAD_DIM = 128
LANES = 128
LOG2E = math.log2(math.e)
F32 = jnp.float32
BF16 = jnp.bfloat16
VMEM = pltpu.VMEM


def passed_along(value, axis, steps):
    count = lax.axis_size(axis)
    initial, last = (max(0, -steps), min(count, count - steps))
    return lax.ppermute(value, axis, [(source, source + steps) for source in range(initial, last)])


def dot_nt(a, b):
    return lax.dot_general(a, b, (((1,), (1,)), ((), ())), preferred_element_type=F32)


def dot_nn(a, b):
    return lax.dot_general(a, b, (((1,), (0,)), ((), ())), preferred_element_type=F32)


def whole(count):
    return [pl.BlockSpec(memory_space=VMEM) for _ in range(count)]


def row_of(column):
    return jnp.transpose(jnp.broadcast_to(column, (column.shape[0], LANES)))[0:1]


def query_kernel(place_ref, own_ref, kv_ref, att_ref, dq_ref, stat_ref, s_ref, p_ref):
    place = place_ref[0]
    ring, strips, _, rows, depth = kv_ref.shape
    span = ring * rows
    factor = HEAD_DIM ** (-0.5) * LOG2E
    line = lax.broadcasted_iota(jnp.int32, (rows, span), 0) + place * rows
    allowed = lax.broadcasted_iota(jnp.int32, (rows, span), 1) <= line
    tops = [None] * strips
    for zk in range(strips):
        key = kv_ref[:, zk, 0].reshape(span, depth)
        query = own_ref[zk:, 0].reshape((strips - zk) * rows, depth)
        scores = dot_nt(query, key) * factor
        for zq in range(zk, strips):
            part = scores[(zq - zk) * rows : (zq - zk + 1) * rows]
            if zq == zk:
                part = jnp.where(allowed, part, -1e30)
            s_ref[zq * rows : (zq + 1) * rows, zk * span : (zk + 1) * span] = part
            top = jnp.max(part, axis=1, keepdims=True)
            tops[zq] = top if zk == 0 else jnp.maximum(tops[zq], top)
    totals = [jnp.zeros((rows, 1), F32) for _ in range(strips)]
    outs = [jnp.zeros((rows, depth), F32) for _ in range(strips)]
    for zk in range(strips):
        columns = slice(zk * span, (zk + 1) * span)
        for zq in range(zk, strips):
            lines = slice(zq * rows, (zq + 1) * rows)
            power = jnp.exp2(s_ref[lines, columns] - tops[zq])
            totals[zq] = totals[zq] + jnp.sum(power, axis=1, keepdims=True)
            p_ref[lines, columns] = power.astype(BF16)
        value = kv_ref[:, zk, 1].reshape(span, depth)
        added = dot_nn(p_ref[zk * rows :, columns], value)
        for zq in range(zk, strips):
            outs[zq] = outs[zq] + added[(zq - zk) * rows : (zq - zk + 1) * rows]
    inverses, deltas = ([], [])
    for zq in range(strips):
        inverse = 1.0 / totals[zq]
        attended = (outs[zq] * inverse).astype(BF16)
        att_ref[zq] = attended
        delta = jnp.sum(
            own_ref[zq, 1].astype(F32) * attended.astype(F32), axis=1, keepdims=True
        )
        stat_ref[zq, 0:1] = row_of(tops[zq] + jnp.log(totals[zq]) * LOG2E)
        stat_ref[zq, 1:2] = row_of(delta)
        inverses.append(inverse)
        deltas.append(delta)
    grads = [jnp.zeros((rows, depth), F32) for _ in range(strips)]
    for zk in range(strips):
        columns = slice(zk * span, (zk + 1) * span)
        key = kv_ref[:, zk, 0].reshape(span, depth)
        value = kv_ref[:, zk, 1].reshape(span, depth)
        out_grad = own_ref[zk:, 1].reshape((strips - zk) * rows, depth)
        dots = dot_nt(out_grad, value)
        parts = []
        for zq in range(zk, strips):
            lines = slice(zq * rows, (zq + 1) * rows)
            here = dots[(zq - zk) * rows : (zq - zk + 1) * rows]
            parts.append((p_ref[lines, columns].astype(F32) * (here - deltas[zq])).astype(BF16))
        added = dot_nn(jnp.concatenate(parts, axis=0), key)
        for zq in range(zk, strips):
            grads[zq] = grads[zq] + added[(zq - zk) * rows : (zq - zk + 1) * rows]
    for zq in range(strips):
        dq_ref[zq] = (grads[zq] * (inverses[zq] * HEAD_DIM ** (-0.5))).astype(BF16)


def key_kernel(place_ref, own_ref, qd_ref, stat_ref, att_ref, dq_ref, out_ref):
    place = place_ref[0]
    ring, strips, _, rows, depth = qd_ref.shape
    span = ring * rows
    factor = HEAD_DIM ** (-0.5) * LOG2E
    line = lax.broadcasted_iota(jnp.int32, (rows, span), 0) + place * rows
    allowed = lax.broadcasted_iota(jnp.int32, (rows, span), 1) >= line
    key_sums = [jnp.zeros((rows, depth), F32) for _ in range(strips)]
    value_sums = [jnp.zeros((rows, depth), F32) for _ in range(strips)]
    for zq in range(strips):
        count = zq + 1
        query = qd_ref[:, zq, 0].reshape(span, depth)
        out_grad = qd_ref[:, zq, 1].reshape(span, depth)
        norm = jnp.concatenate([stat_ref[r, zq, 0:1] for r in range(ring)], axis=1)
        delta = jnp.concatenate([stat_ref[r, zq, 1:2] for r in range(ring)], axis=1)
        key = own_ref[:count, 0].reshape(count * rows, depth)
        value = own_ref[:count, 1].reshape(count * rows, depth)
        scores = dot_nt(key, query) * factor - norm
        last = jnp.where(allowed, scores[zq * rows :], -1e30)
        if zq:
            scores = jnp.concatenate([scores[: zq * rows], last], axis=0)
        else:
            scores = last
        weights = jnp.exp2(scores).astype(BF16)
        dots = dot_nt(value, out_grad)
        score_grad = (weights.astype(F32) * (dots - delta)).astype(BF16)
        value_added = dot_nn(weights, out_grad)
        key_added = dot_nn(score_grad, query)
        for zk in range(count):
            lines = slice(zk * rows, (zk + 1) * rows)
            value_sums[zk] = value_sums[zk] + value_added[lines]
            key_sums[zk] = key_sums[zk] + key_added[lines]
    for zk in range(strips):
        out_ref[zk, 0] = att_ref[zk]
        out_ref[zk, 1] = dq_ref[zk]
        out_ref[zk, 2] = (key_sums[zk] * HEAD_DIM ** (-0.5)).astype(BF16)
        out_ref[zk, 3] = value_sums[zk].astype(BF16)


def fill_phases(first, second, ext_ref, phase_ref):
    rows = first.shape[0]
    ext_ref[:rows] = first
    ext_ref[rows:] = second
    for r in range(8):
        phase_ref[r] = ext_ref[r : r + 2 * rows - 8]


def mix_kernel(
    left_ref, value_ref, before_ref, gate_ref, residual_ref, upstream_ref, taps_ref, skip_ref,
    gain_ref, mixed_ref, stream_ref, sums_ref, ext_ref, phase_ref,
):
    rows = left_ref.shape[0]
    taps = taps_ref.shape[0]
    product = (left_ref[...].astype(F32) * value_ref[...].astype(F32)).astype(BF16).astype(F32)
    fill_phases(before_ref[...].astype(F32), product, ext_ref, phase_ref)
    mixed = (taps_ref[0:1] + skip_ref[...]) * product
    for tap in range(1, taps):
        a, r = divmod(rows - tap, 8)
        mixed = mixed + taps_ref[tap : tap + 1] * phase_ref[r, 8 * a : 8 * a + rows]
    stream = residual_ref[...].astype(F32) + gate_ref[...].astype(F32) * mixed
    mixed_ref[...] = mixed
    stream_ref[...] = stream
    upstream = upstream_ref[...].astype(F32) * gain_ref[...]

    @pl.when(pl.program_id(0) == 0)
    def _():
        sums_ref[...] = jnp.zeros_like(sums_ref)

    sums_ref[0] += stream * stream
    sums_ref[1] += upstream * stream


def norm_kernel(
    upstream_ref, gate_ref, mixed_ref, stream_ref, gain_ref, totals_ref,
    normed_ref, residual_grad_ref, outer_grad_ref, gated_ref, gain_grad_ref, *, width,
):
    inv_rms = lax.rsqrt(totals_ref[:, 0:1] * (1.0 / width) + 1e-06)
    norm_dot = totals_ref[:, 1:2] * inv_rms * (1.0 / width)
    gain = gain_ref[...]
    upstream = upstream_ref[...].astype(F32)
    scaled = stream_ref[...] * inv_rms
    normed_ref[...] = (scaled * gain).astype(BF16)
    gain_grad_ref[...] = jnp.sum(upstream * scaled, axis=0, keepdims=True)
    stream_grad = inv_rms * (upstream * gain - scaled * norm_dot)
    residual_grad_ref[...] = stream_grad.astype(BF16)
    outer_grad_ref[...] = (stream_grad * mixed_ref[...]).astype(BF16)
    gated_ref[...] = (stream_grad * gate_ref[...].astype(F32)).astype(BF16)


def back_kernel(
    left_ref, value_ref, before_ref, gated_ref, after_ref, taps_ref, skip_ref,
    left_grad_ref, value_grad_ref, filter_ref, skip_grad_ref, ext_ref, phase_ref,
):
    rows = left_ref.shape[0]
    taps = taps_ref.shape[0]
    left = left_ref[...].astype(F32)
    value = value_ref[...].astype(F32)
    product = (left * value).astype(BF16).astype(F32)
    gated = gated_ref[...].astype(F32)
    fill_phases(gated, after_ref[...].astype(F32), ext_ref, phase_ref)
    grad = (skip_ref[...] + taps_ref[0:1]) * gated
    for tap in range(1, taps):
        a, r = divmod(tap, 8)
        grad = grad + taps_ref[tap : tap + 1] * phase_ref[r, 8 * a : 8 * a + rows]
    left_grad_ref[...] = (grad * value).astype(BF16)
    value_grad_ref[...] = (grad * left).astype(BF16)
    fill_phases(before_ref[...].astype(F32), product, ext_ref, phase_ref)
    direct = jnp.sum(gated * product, axis=0, keepdims=True)
    skip_grad_ref[...] = direct
    filter_ref[0:1] = direct
    for tap in range(1, taps):
        a, r = divmod(rows - tap, 8)
        filter_ref[tap : tap + 1] = jnp.sum(
            gated * phase_ref[r, 8 * a : 8 * a + rows], axis=0, keepdims=True
        )


def pack_kernel(key_ref, value_ref, query_ref, grad_ref, kv_ref, qd_ref):
    for h in range(kv_ref.shape[0]):
        columns = slice(h * HEAD_DIM, (h + 1) * HEAD_DIM)
        kv_ref[h, 0] = key_ref[:, columns]
        kv_ref[h, 1] = value_ref[:, columns]
        qd_ref[h, 0] = query_ref[:, columns]
        qd_ref[h, 1] = grad_ref[:, columns]


def unpack_kernel(in_ref, *refs):
    for h in range(in_ref.shape[0]):
        for number, ref in enumerate(refs):
            ref[:, h * HEAD_DIM : (h + 1) * HEAD_DIM] = in_ref[h, number]


def exchange_kernel(x_ref, out_ref, slots_ref, send_sem, recv_sem, *, team, summed):
    count = slots_ref.shape[0]
    me, device = team()
    barrier = pltpu.get_barrier_semaphore()
    for step in range(1, count):
        pl.semaphore_signal(
            barrier,
            inc=1,
            device_id=device(lax.rem(me + step, count)),
            device_id_type=pl.DeviceIdType.MESH,
        )
    slots_ref[me] = x_ref[...]
    pl.semaphore_wait(barrier, count - 1)
    copies = []
    for step in range(1, count):
        copy = pltpu.make_async_remote_copy(
            src_ref=x_ref,
            dst_ref=slots_ref.at[me],
            send_sem=send_sem.at[step - 1],
            recv_sem=recv_sem.at[step - 1],
            device_id=device(lax.rem(me + step, count)),
            device_id_type=pl.DeviceIdType.MESH,
        )
        copy.start()
        copies.append(copy)
    for copy in copies:
        copy.wait()
    if summed:
        total = slots_ref[0]
        for slot in range(1, count):
            total = total + slots_ref[slot]
        out_ref[...] = total
    else:
        out_ref[...] = slots_ref[...]


def exchange(x, count, team, summed, number, name):
    return pl.pallas_call(
        lambda *refs: exchange_kernel(*refs, team=team, summed=summed),
        in_specs=whole(1),
        out_specs=whole(1)[0],
        out_shape=shape_of(x.shape if summed else (count, *x.shape), x.dtype),
        scratch_shapes=[
            VMEM((count, *x.shape), x.dtype),
            pltpu.SemaphoreType.DMA((count - 1,)),
            pltpu.SemaphoreType.DMA((count - 1,)),
        ],
        compiler_params=pltpu.CompilerParams(collective_id=number, has_side_effects=True),
        name=name,
    )(x)


def shape_of(shape, dtype):
    return jax.ShapeDtypeStruct(shape, dtype)


def shards(
    left_stream,
    outer_gate,
    value_stream,
    residual,
    long_filter,
    skip_weight,
    norm_gain,
    normed_grad,
    attn_queries,
    attn_keys,
    attn_values,
    attended_grad,
):
    rows = left_stream.shape[1]
    channels = left_stream.shape[2]
    groups, taps = long_filter.shape
    per_group = channels // groups
    width = channels * lax.axis_size("tp")
    heads = attn_queries.shape[2] // HEAD_DIM
    devices = lax.axis_size("ctx")
    ring = devices // heads
    index = lax.axis_index("ctx")
    place = (index % ring).astype(jnp.int32).reshape(1)
    across = [[strip * ring + spot for strip in range(heads)] for spot in range(ring)]
    along = [[strip * ring + spot for spot in range(ring)] for strip in range(heads)]

    lanes = lax.axis_size("tp")
    strips = devices // ring

    def over_tp():
        return lax.axis_index("tp"), lambda peer: {"tp": peer}

    def over_ring():
        here = lax.axis_index("ctx")
        first = here // ring * ring
        return here % ring, lambda peer: {"ctx": first + peer}

    def over_strips():
        here = lax.axis_index("ctx")
        spot = here % ring
        me = lax.axis_index("dp") * strips + here // ring
        return me, lambda peer: {"dp": peer // strips, "ctx": peer % strips * ring + spot}

    pair = shape_of((heads, 2, rows, HEAD_DIM), BF16)
    send_kv, send_qd = pl.pallas_call(
        pack_kernel,
        in_specs=whole(4),
        out_specs=whole(2),
        out_shape=[pair, pair],
        name="pack",
    )(attn_keys[0], attn_values[0], attn_queries[0], attended_grad[0])
    own_kv = lax.all_to_all(send_kv, "ctx", 0, 0, axis_index_groups=across, tiled=True)
    all_kv = lax.all_gather(own_kv, "ctx", axis=0, axis_index_groups=along, tiled=False)
    own_kv, send_qd = lax.optimization_barrier((own_kv, send_qd))
    own_qd = lax.all_to_all(send_qd, "ctx", 0, 0, axis_index_groups=across, tiled=True)
    all_qd = lax.all_gather(own_qd, "ctx", axis=0, axis_index_groups=along, tiled=False)

    own_qd, left_stream = lax.optimization_barrier((own_qd, left_stream))
    left, value, gate = (left_stream[0], value_stream[0], outer_gate[0])
    upstream = normed_grad[0]
    product = (left.astype(F32) * value.astype(F32)).astype(BF16)
    before = passed_along(product, "ctx", 1)
    taps_rows = jnp.repeat(long_filter.T, per_group, axis=1)
    skip, gain = (skip_weight[None, :], norm_gain[None, :])
    grid = (channels // LANES,)
    block = pl.BlockSpec((rows, LANES), lambda j: (0, j))
    tap_block = pl.BlockSpec((taps, LANES), lambda j: (0, j))
    line = pl.BlockSpec((1, LANES), lambda j: (0, j))
    phases = [VMEM((2 * rows, LANES), F32), VMEM((8, 2 * rows - 8, LANES), F32)]
    size = rows * channels
    mixed, stream, sums = pl.pallas_call(
        mix_kernel,
        grid=grid,
        in_specs=[block] * 6 + [tap_block, line, line],
        out_specs=[block, block, pl.BlockSpec((2, rows, LANES), lambda j: (0, 0, 0))],
        out_shape=[
            shape_of((rows, channels), F32),
            shape_of((rows, channels), F32),
            shape_of((2, rows, LANES), F32),
        ],
        scratch_shapes=phases,
        cost_estimate=pl.CostEstimate(
            flops=2 * taps * size, bytes_accessed=20 * size, transcendentals=0
        ),
        name="mix",
    )(left, value, before, gate, residual[0], upstream, taps_rows, skip, gain)
    totals = exchange(jnp.sum(sums, axis=2), lanes, over_tp, True, 0, "tp_sums").T
    normed, grad_residual, grad_outer, gated, gain_part = pl.pallas_call(
        lambda *refs: norm_kernel(*refs, width=width),
        in_specs=whole(6),
        out_specs=whole(5),
        out_shape=[shape_of((rows, channels), BF16)] * 4 + [shape_of((1, channels), F32)],
        cost_estimate=pl.CostEstimate(
            flops=20 * size, bytes_accessed=20 * size, transcendentals=0
        ),
        name="norm",
    )(upstream, gate, mixed, stream, gain, totals)
    after = passed_along(gated, "ctx", -1)
    grad_left, grad_value, filter_rows, skip_part = pl.pallas_call(
        back_kernel,
        grid=grid,
        in_specs=[block] * 5 + [tap_block, line],
        out_specs=[block, block, tap_block, line],
        out_shape=[
            shape_of((rows, channels), BF16),
            shape_of((rows, channels), BF16),
            shape_of((taps, channels), F32),
            shape_of((1, channels), F32),
        ],
        scratch_shapes=phases,
        cost_estimate=pl.CostEstimate(
            flops=4 * taps * size, bytes_accessed=20 * size, transcendentals=0
        ),
        name="back",
    )(left, value, before, gated, after, taps_rows, skip)
    member = (
        jnp.arange(channels, dtype=jnp.int32)[None, :] // per_group
        == jnp.arange(groups, dtype=jnp.int32)[:, None]
    ).astype(F32)
    filter_part = lax.dot_general(
        member, filter_rows, (((1,), (1,)), ((), ())), precision=lax.Precision.HIGHEST
    )
    small = jnp.concatenate(
        [filter_part.reshape(-1), skip_part.reshape(-1), gain_part.reshape(-1)]
    )
    small, own_qd = lax.optimization_barrier((small.reshape(-1, LANES), own_qd))

    smem = pl.BlockSpec(memory_space=pltpu.SMEM)
    blocks = (heads, rows, HEAD_DIM)
    pairs = heads * (heads + 1) // 2 * rows * ring * rows
    attended, grad_queries, stats = pl.pallas_call(
        query_kernel,
        in_specs=[smem] + whole(2),
        out_specs=whole(3),
        out_shape=[shape_of(blocks, BF16), shape_of(blocks, BF16), shape_of((heads, 2, rows), F32)],
        scratch_shapes=[
            VMEM((heads * rows, devices * rows), F32),
            VMEM((heads * rows, devices * rows), BF16),
        ],
        cost_estimate=pl.CostEstimate(
            flops=8 * HEAD_DIM * pairs, bytes_accessed=3 << 20, transcendentals=pairs
        ),
        name="query",
    )(place, own_qd, all_kv)
    lines = 2 * heads
    gathered = exchange(
        jnp.concatenate([stats.reshape(lines, rows), small], axis=0),
        ring, over_ring, False, 1, "ring_gather",
    )
    all_stats = gathered[:, :lines].reshape(ring, heads, 2, rows)
    small = exchange(
        jnp.sum(gathered[:, lines:], axis=0),
        strips * lax.axis_size("dp"), over_strips, True, 2, "strip_sums",
    )
    small, own_kv = lax.optimization_barrier((small, own_kv))
    small = small.reshape(-1)
    cut = groups * taps
    filter_sum = small[:cut].reshape(groups, taps)
    skip_sum, gain_sum = (small[cut : cut + channels], small[cut + channels :])
    back = pl.pallas_call(
        key_kernel,
        in_specs=[smem] + whole(5),
        out_specs=whole(1)[0],
        out_shape=shape_of((heads, 4, rows, HEAD_DIM), BF16),
        cost_estimate=pl.CostEstimate(
            flops=8 * HEAD_DIM * pairs, bytes_accessed=3 << 20, transcendentals=pairs
        ),
        name="key",
    )(place, own_kv, all_qd, all_stats, attended, grad_queries)
    back = lax.all_to_all(back, "ctx", 0, 0, axis_index_groups=across, tiled=True)
    back = pl.pallas_call(
        unpack_kernel,
        in_specs=whole(1),
        out_specs=whole(4),
        out_shape=[shape_of((rows, heads * HEAD_DIM), BF16)] * 4,
        name="unpack",
    )(back)
    return (
        normed[None],
        grad_left[None],
        grad_outer[None],
        grad_value[None],
        grad_residual[None],
        filter_sum,
        skip_sum,
        gain_sum,
        back[0][None],
        back[1][None],
        back[2][None],
        back[3][None],
    )


def solution(mesh):
    in_specs = (
        P("dp", "ctx", "tp"),
        P("dp", "ctx", "tp"),
        P("dp", "ctx", "tp"),
        P("dp", "ctx", "tp"),
        P("tp", None),
        P("tp"),
        P("tp"),
        P("dp", "ctx", "tp"),
        P("dp", "ctx", "tp"),
        P("dp", "ctx", "tp"),
        P("dp", "ctx", "tp"),
        P("dp", "ctx", "tp"),
    )
    out_specs = (
        P("dp", "ctx", "tp"),
        P("dp", "ctx", "tp"),
        P("dp", "ctx", "tp"),
        P("dp", "ctx", "tp"),
        P("dp", "ctx", "tp"),
        P("tp", None),
        P("tp"),
        P("tp"),
        P("dp", "ctx", "tp"),
        P("dp", "ctx", "tp"),
        P("dp", "ctx", "tp"),
        P("dp", "ctx", "tp"),
    )
    return jax.shard_map(shards, mesh=mesh, in_specs=in_specs, out_specs=out_specs, check_vma=False)
```
